256 devices in a mesh: dp: 4 (over y), seq: 16 (over z, core), fsdp: 4 (over x).
Axes of the slice: x: 4, y: 4, z: 8, core: 2. Of those that a mesh axis runs over, the one named last changes fastest.
Arguments:
- signal: bfloat16 [16, 2048, 1024], P(('dp', 'fsdp'), 'seq'), may hold values from -100 to 100
- w_query: bfloat16 [1024, 512], P('fsdp'), may hold values from -1 to 1
- w_key: bfloat16 [1024, 512], P('fsdp'), may hold values from -1 to 1
- w_value: bfloat16 [1024, 512], P('fsdp'), may hold values from -0.1875 to 0.1875
- w_output: bfloat16 [1024, 512], P('fsdp'), may hold values from -0.25 to 0.25
- upstream: bfloat16 [16, 2048, 1024], P(('dp', 'fsdp'), 'seq'), may hold values from -6 to 6
Outputs:
- output: bfloat16 [16, 2048, 1024], P(('dp', 'fsdp'), 'seq')
- grad_signal: bfloat16 [16, 2048, 1024], P(('dp', 'fsdp'), 'seq')
- grad_query: float32 [1024, 512], P('fsdp')
- grad_key: float32 [1024, 512], P('fsdp')
- grad_value: float32 [1024, 512], P('fsdp')
- grad_output: float32 [1024, 512], P('fsdp')
The draws below stay inside these ranges and needn't reach their ends.
All inputs are finite; a program needn't handle non-finite values.
Results may differ from the reference program's by a relative error of at most 0.02.
The reference program's roundings to bfloat16 on the way (of `normed`, `queries`, `attn_weights`, `context`, `grad_context`, `grad_scores` and `grad_keys`) count: a program that leaves them out, or rounds other values in their place, can miss the bound.
Values may be sent and summed in bfloat16 or wider, within the bound.
No kernel may reach another device: no remote copies, remote signals or barrier semaphores. Data moves between devices by JAX's collectives and lax.ppermute only.
A program may use at most 128 MiB of HBM per device.

```python
import math
import jax
import jax.numpy as jnp
from jax import lax

D = 1024
HEADS = 8
HSIZE = 64
FR_DEV = 128
HD = 512
FRAMES = 2048
RECORDS = 16
TOKENS = 32768


def draw_signal(key, part):
    shape = (RECORDS, FRAMES, D)
    col_scale = jnp.exp(jax.random.uniform(jax.random.fold_in(key, 32), (D,), jnp.float32, math.log(0.3), math.log(3.0)))
    row_scale = jnp.exp(jax.random.uniform(jax.random.fold_in(key, 33), (RECORDS, FRAMES, 1), jnp.float32, math.log(0.5), math.log(1.5)))
    blocks = FRAMES // FR_DEV
    block_width = D // blocks
    order = jax.random.permutation(jax.random.fold_in(key, 34), blocks)
    frame_block = jnp.arange(FRAMES) // FR_DEV
    col_block = jnp.arange(D) // block_width
    target = (order[frame_block][None, :] + jnp.arange(RECORDS)[:, None]) % blocks
    boost = jnp.where(col_block[None, None, :] == target[:, :, None], 2.0, 1.0)
    noise = jax.random.truncated_normal(jax.random.fold_in(key, 31), -4.0, 4.0, shape, jnp.float32)
    base = noise * col_scale * boost
    return (base * row_scale).astype(jnp.bfloat16)


def draw_w_query(key, part):
    base = jax.random.truncated_normal(jax.random.fold_in(key, 21), -4.0, 4.0, (D, HD), jnp.float32) * (1.7 / math.sqrt(D))
    return base.astype(jnp.bfloat16)


def draw_w_key(key, part):
    base = jax.random.truncated_normal(jax.random.fold_in(key, 22), -4.0, 4.0, (D, HD), jnp.float32) * (1.7 / math.sqrt(D))
    return base.astype(jnp.bfloat16)


def level_of(stream_key, shape, split, low, top_value):
    gain = 1.0
    for axis_at, blocks in split:
        heights = jax.random.uniform(jax.random.fold_in(jax.random.fold_in(stream_key, 6), axis_at), (blocks,), jnp.float32, low / len(split), top_value / len(split))
        gain = gain * jnp.repeat(jnp.exp(heights), shape[axis_at] // blocks).reshape((-1,) + (1,) * (len(shape) - 1 - axis_at))
    return gain


def centred(key, shape, deviation, most, shards=(), dtype=jnp.bfloat16):
    drawn = deviation * jax.random.normal(key, shape, jnp.float32)
    if shards:
        drawn = drawn * level_of(key, shape, shards, -0.22, 0.18)
    return jnp.clip(drawn, -most, most).astype(dtype)


def setup_inputs(seed: int = 0) -> dict:
    streams_of = jax.random.split(jax.random.key(seed), 7)
    signal = draw_signal(jax.random.fold_in(streams_of[6], 71), 0)
    w_query = draw_w_query(jax.random.fold_in(streams_of[6], 71), 0)
    w_key = draw_w_key(jax.random.fold_in(streams_of[6], 71), 0)
    w_value = centred(streams_of[3], (D, HD), D ** -0.5, 0.1875, ((0, 4),))
    w_output = centred(streams_of[4], (D, HD), HD ** -0.5, 0.25, ((0, 4),))
    upstream = centred(streams_of[5], (RECORDS, FRAMES, D), 1.0, 6.0, ((0, 16), (1, 16)))
    return {"signal": signal, "w_query": w_query, "w_key": w_key, "w_value": w_value, "w_output": w_output, "upstream": upstream}


def normalize(frame_rows):
    widened = frame_rows.astype(jnp.float32)
    centre = widened - lax.optimization_barrier(jnp.mean(widened, axis=-1, keepdims=True))
    variance = lax.optimization_barrier(jnp.mean(centre * centre, axis=-1, keepdims=True))
    inverse = lax.rsqrt(variance + 1e-05)
    return (centre * inverse, inverse)

def split_heads(matrix):
    return matrix.reshape(matrix.shape[0], HEADS, HSIZE).astype(jnp.float32)

def reference(signal, w_query, w_key, w_value, w_output, upstream):
    score_scale = HSIZE ** (-0.5)

    def record(record_pair):
        frame_rows, grad_frames = record_pair
        normed_f, inverse = normalize(frame_rows)
        normed = normed_f.astype(jnp.bfloat16)
        queries = jnp.dot(normed, w_query, preferred_element_type=jnp.float32).astype(jnp.bfloat16)
        key_rows = jnp.dot(normed, w_key, preferred_element_type=jnp.float32).astype(jnp.bfloat16)
        value_rows = jnp.dot(normed, w_value, preferred_element_type=jnp.float32).astype(jnp.bfloat16)
        query_heads = split_heads(queries)
        key_heads = split_heads(key_rows)
        value_heads = split_heads(value_rows)
        scores = jnp.einsum('qhs,khs->hqk', query_heads, key_heads) * score_scale
        row_max = lax.optimization_barrier(jnp.max(scores, axis=-1, keepdims=True))
        exponent = jnp.exp(scores - row_max)
        attention = exponent / lax.optimization_barrier(jnp.sum(exponent, axis=-1, keepdims=True))
        attn_weights = attention.astype(jnp.bfloat16)
        context = jnp.einsum('hqk,khs->qhs', attn_weights.astype(jnp.float32), value_heads)
        context = context.reshape(FRAMES, HD).astype(jnp.bfloat16)
        projected = jnp.dot(context, w_output.T, preferred_element_type=jnp.float32)
        output_rows = (frame_rows.astype(jnp.float32) + projected).astype(jnp.bfloat16)
        grad_context = jnp.dot(grad_frames, w_output, preferred_element_type=jnp.float32).astype(jnp.bfloat16)
        grad_heads = split_heads(grad_context)
        grad_attention = jnp.einsum('qhs,khs->hqk', grad_heads, value_heads)
        row_delta = lax.optimization_barrier(jnp.sum(attention * grad_attention, axis=-1, keepdims=True))
        grad_scores = (attention * (grad_attention - row_delta) * score_scale).astype(jnp.bfloat16)
        wide_scores = grad_scores.astype(jnp.float32)
        grad_queries = jnp.einsum('hqk,khs->qhs', wide_scores, key_heads).reshape(FRAMES, HD).astype(jnp.bfloat16)
        grad_keys = jnp.einsum('hqk,qhs->khs', wide_scores, query_heads).reshape(FRAMES, HD).astype(jnp.bfloat16)
        grad_values = jnp.einsum('hqk,qhs->khs', attn_weights.astype(jnp.float32), grad_heads)
        grad_values = grad_values.reshape(FRAMES, HD).astype(jnp.bfloat16)
        grad_normed = jnp.dot(grad_queries, w_query.T, preferred_element_type=jnp.float32)
        grad_normed = grad_normed + jnp.dot(grad_keys, w_key.T, preferred_element_type=jnp.float32)
        grad_normed = grad_normed + jnp.dot(grad_values, w_value.T, preferred_element_type=jnp.float32)
        grad_mean = lax.optimization_barrier(jnp.mean(grad_normed, axis=-1, keepdims=True))
        grad_along = lax.optimization_barrier(jnp.mean(grad_normed * normed_f, axis=-1, keepdims=True))
        grad_rows = grad_frames.astype(jnp.float32) + inverse * (grad_normed - grad_mean - normed_f * grad_along)
        grad_rows = grad_rows.astype(jnp.bfloat16)
        terms = jnp.concatenate([jnp.dot(normed.T, grad_queries, preferred_element_type=jnp.float32), jnp.dot(normed.T, grad_keys, preferred_element_type=jnp.float32), jnp.dot(normed.T, grad_values, preferred_element_type=jnp.float32), jnp.dot(grad_frames.T, context, preferred_element_type=jnp.float32)], axis=1)
        return (output_rows, grad_rows, terms)
    output_rows, grad_rows, terms = lax.map(record, (signal, upstream))
    totals = lax.optimization_barrier(jnp.sum(terms, axis=0)) * TOKENS ** (-0.5)
    return (output_rows, grad_rows, totals[:, :HD], totals[:, HD:2 * HD], totals[:, 2 * HD:3 * HD], totals[:, 3 * HD:])
```

```python
import jax
import jax.numpy as jnp
from jax import lax
from jax.experimental import pallas as pl
from jax.experimental.pallas import tpu as pltpu
from jax.sharding import Mesh
from jax.sharding import PartitionSpec as P


HSIZE = 64
LOG2E = 1.4426950408889634
F32 = jnp.float32
BF16 = jnp.bfloat16


def vmem(count):
    return [pl.BlockSpec(memory_space=pltpu.VMEM) for _ in range(count)]


def smem():
    return pl.BlockSpec(memory_space=pltpu.SMEM)


def call(kernel, ids, args, outs, scratch=()):
    return pl.pallas_call(
        kernel,
        in_specs=[smem()] + vmem(len(args)),
        out_specs=vmem(len(outs)),
        out_shape=[jax.ShapeDtypeStruct(s, d) for s, d in outs],
        scratch_shapes=list(scratch),
    )(ids, *args)


def normalize(rows):
    wide = rows.astype(F32)
    centre = wide - jnp.mean(wide, axis=-1, keepdims=True)
    variance = jnp.mean(centre * centre, axis=-1, keepdims=True)
    inverse = lax.rsqrt(variance + 1e-05)
    return centre * inverse, inverse


def dot(a, b, dims):
    return lax.dot_general(a, b, (dims, ((), ())), preferred_element_type=F32)


def low_lanes(shape):
    return lax.broadcasted_iota(jnp.int32, shape, len(shape) - 1) < HSIZE


def shift(value, axis, size, by):
    return lax.ppermute(value, axis, [(i, (i + by) % size) for i in range(size)])


def block_of(ids, step):
    return pl.multiple_of(lax.rem(ids[1] + step, 4) * 256, 256)


def project_kernel(ids, own_sig, oth_sig, own_up, oth_up, w0, w1, w2a, w2b, w3, heads, first, second):
    core = ids[0]
    for half, (sig, up) in enumerate(((own_sig, own_up), (oth_sig, oth_up))):
        rows = pl.ds(half * 128, 128)
        normed = normalize(sig[...])[0].astype(BF16)
        first[rows, :] = normed
        second[rows, :] = jnp.where(core == 0, normed, up[...])
    one = two = None
    for step, piece in enumerate((w0, w1, (w2a, w2b), w3)):
        cols = pl.ds(block_of(ids, step), 256)
        if step == 2:
            weight = jnp.concatenate([piece[0][...], piece[1][...]], axis=0)
        else:
            weight = piece[...]
        a = dot(first[:, cols], weight[:, :512], ((1,), (0,)))
        b = dot(second[:, cols], weight[:, 512:], ((1,), (0,)))
        one = a if one is None else one + a
        two = b if two is None else two + b
    mask = low_lanes((256, 128))
    for pair in range(4):
        lanes = slice(128 * pair, 128 * pair + 128)
        t1, t2 = one[:, lanes], two[:, lanes]
        heads[2 * pair] = jnp.where(mask, t1, pltpu.roll(t2, 64, 1)).astype(BF16)
        heads[2 * pair + 1] = jnp.where(mask, pltpu.roll(t1, 64, 1), t2).astype(BF16)


def attention_kernel(ids, own, other, send, keep, kv, qg, acc):
    core = ids[0]
    keys, block = kv.shape[0], 256

    @pl.when(core == 0)
    def _():
        kv[...] = own[...]
        qg[...] = other[0:1024, :]

    @pl.when(core != 0)
    def _():
        kv[...] = other[...]
        qg[...] = own[1024:2048, :]

    low = low_lanes((keys, 128))
    zero = jnp.zeros((), BF16)
    pairs = kv[...]
    key_rows = jnp.where(low, pairs, zero)
    value_rows = jnp.where(low, zero, pairs)
    key_cols = key_rows.astype(F32).T.astype(BF16)
    value_cols = value_rows.astype(F32).T.astype(BF16)
    low_q = low_lanes((block, 128))
    scale = jnp.where(low_lanes((1, 128)), HSIZE**-0.5, 1.0).astype(F32)
    acc[...] = jnp.zeros_like(acc)

    def step(i, carry):
        rows = pl.ds(pl.multiple_of(i * block, block), block)
        qb = qg[rows, :]
        s = dot(key_rows, qb, ((1,), (1,)))
        top = jnp.max(s, axis=0, keepdims=True)
        e = jnp.exp2((s - top) * (HSIZE**-0.5 * LOG2E))
        inv = 1.0 / jnp.sum(e, axis=0, keepdims=True)
        att = e * inv
        grad = dot(value_rows, qb, ((1,), (1,)))
        delta = jnp.sum(att * grad, axis=0, keepdims=True)
        weights = att.astype(BF16)
        gs = (att * (grad - delta)).astype(BF16)
        qk = jnp.where(low_q, qb, zero)
        qv = jnp.where(low_q, zero, qb)
        acc[...] += dot(gs, qk, ((1,), (0,))) + dot(weights, qv, ((1,), (0,)))
        turned = dot(key_cols, gs, ((1,), (0,))) + dot(value_cols, weights, ((1,), (0,)))
        result = (turned.T * scale).astype(BF16)

        @pl.when(core == 0)
        def _():
            send[rows, :] = result

        @pl.when(core != 0)
        def _():
            keep[pl.ds(pl.multiple_of(1024 + i * block, block), block), :] = result.astype(F32)

        return carry

    lax.fori_loop(0, 1024 // block, step, 0)

    @pl.when(core == 0)
    def _():
        keep[...] = acc[...] * scale
        send[1024:2048, :] = jnp.zeros((1024, 128), BF16)

    @pl.when(core != 0)
    def _():
        send[...] = (acc[...] * scale).astype(BF16)
        keep[0:1024, :] = jnp.zeros((1024, 128), F32)


def unpack(heads):
    mask = low_lanes((256, 128))
    one, two = [], []
    for pair in range(4):
        a, b = heads[2 * pair].astype(F32), heads[2 * pair + 1].astype(F32)
        one.append(jnp.where(mask, a, pltpu.roll(b, 64, 1)).astype(BF16))
        two.append(jnp.where(mask, pltpu.roll(a, 64, 1), b).astype(BF16))
    return jnp.concatenate(one, axis=1), jnp.concatenate(two, axis=1)


def outer_kernel(ids, heads, first, second, shares, g1, g2):
    one, two = unpack(heads)
    g1[...] = one
    g2[...] = two
    for part in range(4):
        cols = slice(256 * part, 256 * part + 256)
        shares[part, :, :512] = dot(first[:, cols], one, ((0,), (0,))).astype(BF16)
        shares[part, :, 512:] = dot(second[:, cols], two, ((0,), (0,))).astype(BF16)


def back_kernel(ids, g1, g2, w0, w1, w2a, w2b, w3, keep, send):
    core = ids[0]
    for step, piece in enumerate((w0, w1, (w2a, w2b), w3)):
        cols = pl.ds(block_of(ids, step), 256)
        if step == 2:
            weight = jnp.concatenate([piece[0][...], piece[1][...]], axis=0)
        else:
            weight = piece[...]
        a = dot(g1[...], weight[:, :512], ((1,), (1,)))
        b = dot(g2[...], weight[:, 512:], ((1,), (1,)))
        total = jnp.where(core == 0, a + b, a)
        keep[0, :, cols] = total[:128]
        keep[1, :, cols] = jnp.where(core == 0, 0.0, b[:128])
        send[0, :, cols] = total[128:]
        send[1, :, cols] = jnp.where(core == 0, 0.0, b[128:])


def finish_kernel(ids, sig, up, keep, recv, out, grad):
    normed_f, inverse = normalize(sig[...])
    out[...] = (sig[...].astype(F32) + keep[1] + recv[1]).astype(BF16)
    gn = keep[0] + recv[0]
    mean = jnp.mean(gn, axis=-1, keepdims=True)
    along = jnp.mean(gn * normed_f, axis=-1, keepdims=True)
    grad[...] = (up[...].astype(F32) + inverse * (gn - mean - normed_f * along)).astype(BF16)


def exchange(value, axis):
    return lax.all_to_all(value, axis, split_axis=0, concat_axis=0, tiled=True)


def body(signal, w_query, w_key, w_value, w_output, upstream):
    core, place = lax.axis_index("core"), lax.axis_index("fsdp")
    ids = jnp.stack([core, place]).astype(jnp.int32)
    sig, up = signal[0], upstream[0]
    w0 = jnp.concatenate(
        [jnp.where(core == 0, w_key, w_query), jnp.where(core == 0, w_value, w_output)], axis=1
    )
    w1 = shift(w0, "fsdp", 4, -1)
    w3 = shift(w0, "fsdp", 4, 1)
    oth_sig, oth_up = shift(sig, "core", 2, 1), shift(up, "core", 2, 1)
    w2a = shift(w1[:128], "fsdp", 4, -1)
    w2b = shift(w3[128:], "fsdp", 4, 1)
    weights = [w0, w1, w2a, w2b, w3]
    heads, first, second = call(
        project_kernel,
        ids,
        [sig, oth_sig, up, oth_up] + weights,
        [((8, 256, 128), BF16), ((256, 1024), BF16), ((256, 1024), BF16)],
    )
    mine = exchange(heads, "z").reshape(2048, 128)
    other = shift(mine, "core", 2, 1)
    send, keep = call(
        attention_kernel,
        ids,
        [mine, other],
        [((2048, 128), BF16), ((2048, 128), F32)],
        [pltpu.VMEM((2048, 128), BF16), pltpu.VMEM((1024, 128), BF16), pltpu.VMEM((2048, 128), F32)],
    )
    recv = shift(send, "core", 2, 1)
    grads = (keep + recv.astype(F32)).astype(BF16).reshape(8, 256, 128)
    grads = exchange(grads, "z")
    shares, g1, g2 = call(
        outer_kernel,
        ids,
        [grads, first, second],
        [((4, 256, 1024), BF16), ((256, 512), BF16), ((256, 512), BF16)],
    )
    kept, sent = call(
        back_kernel,
        ids,
        [g1, g2] + weights,
        [((2, 128, 1024), F32), ((2, 128, 1024), F32)],
    )
    got = shift(sent, "core", 2, 1)
    out, grad = call(
        finish_kernel,
        ids,
        [sig, up, kept, got],
        [((128, 1024), BF16), ((128, 1024), BF16)],
    )
    total = jnp.sum(exchange(shares, "fsdp").astype(F32), axis=0).astype(BF16)
    total = jnp.sum(exchange(total.reshape(4, 64, 1024), "dp").astype(F32), axis=0).astype(BF16)
    total = jnp.sum(exchange(total.reshape(8, 8, 1024), "z").astype(F32), axis=0).astype(BF16)
    total = exchange(jnp.broadcast_to(total[None], (8, 8, 1024)), "z").reshape(64, 1024)
    total = exchange(jnp.broadcast_to(total[None], (4, 64, 1024)), "dp").reshape(256, 1024)
    across = shift(total, "core", 2, 1)
    kv_part = jnp.where(core == 0, total, across).astype(F32) * 32768**-0.5
    qo_part = jnp.where(core == 0, across, total).astype(F32) * 32768**-0.5
    return (
        out[None],
        grad[None],
        qo_part[:, :512],
        kv_part[:, :512],
        kv_part[:, 512:],
        qo_part[:, 512:],
    )


def solution(mesh):
    dp, seq, fsdp = mesh.devices.shape
    split = Mesh(mesh.devices.reshape(dp, seq // 2, 2, fsdp), ("dp", "z", "core", "fsdp"))
    frames = P(("dp", "fsdp"), ("z", "core"), None)
    rows = P("fsdp", None)
    return jax.shard_map(
        body,
        mesh=split,
        in_specs=(frames, rows, rows, rows, rows, frames),
        out_specs=(frames, frames, rows, rows, rows, rows),
        check_vma=False,
    )
```

```python
import jax
import jax.numpy as jnp
from jax import lax
from jax.experimental import pallas as pl
from jax.experimental.pallas import tpu as pltpu
from jax.sharding import Mesh
from jax.sharding import PartitionSpec as P


HSIZE = 64
LOG2E = 1.4426950408889634
F32 = jnp.float32
BF16 = jnp.bfloat16


def vmem(count):
    return [pl.BlockSpec(memory_space=pltpu.VMEM) for _ in range(count)]


def smem():
    return pl.BlockSpec(memory_space=pltpu.SMEM)


def call(kernel, ids, args, outs, scratch=()):
    return pl.pallas_call(
        kernel,
        in_specs=[smem()] + vmem(len(args)),
        out_specs=vmem(len(outs)),
        out_shape=[jax.ShapeDtypeStruct(s, d) for s, d in outs],
        scratch_shapes=list(scratch),
    )(ids, *args)


def normalize(rows):
    wide = rows.astype(F32)
    centre = wide - jnp.mean(wide, axis=-1, keepdims=True)
    variance = jnp.mean(centre * centre, axis=-1, keepdims=True)
    inverse = lax.rsqrt(variance + 1e-05)
    return centre * inverse, inverse


def dot(a, b, dims):
    return lax.dot_general(a, b, (dims, ((), ())), preferred_element_type=F32)


def low_lanes(shape):
    return lax.broadcasted_iota(jnp.int32, shape, len(shape) - 1) < HSIZE


def shift(value, axis, size, by):
    return lax.ppermute(value, axis, [(i, (i + by) % size) for i in range(size)])


def pair(value):
    return shift(value, "core", 2, 1)


def block_of(ids, step):
    return pl.multiple_of(lax.rem(ids[1] + step, 4) * 256, 256)


def stack_kernel(ids, sig, up, both):
    both[0] = normalize(sig[...])[0].astype(BF16)
    both[1] = up[...]


def whole_weight(piece):
    return jnp.concatenate([part[...] for part in piece], axis=0)


def project_kernel(ids, own, oth, w0t, w0b, w1t, w1b, w2t, w2b, w3t, w3b, heads, first, second):
    core = ids[0]
    for half, both in enumerate((own, oth)):
        at = core if half == 0 else 1 - core
        rows = pl.ds(pl.multiple_of(at * 128, 128), 128)
        first[rows, :] = both[0]
        second[rows, :] = jnp.where(core == 0, both[0], both[1])
    one = two = None
    for step, piece in enumerate(((w0t, w0b), (w1t, w1b), (w2t, w2b), (w3t, w3b))):
        cols = pl.ds(block_of(ids, step), 256)
        weight = whole_weight(piece)
        a = dot(first[:, cols], weight[:, :512], ((1,), (0,)))
        b = dot(second[:, cols], weight[:, 512:], ((1,), (0,)))
        one = a if one is None else one + a
        two = b if two is None else two + b
    mask = low_lanes((256, 128))
    for pair in range(4):
        lanes = slice(128 * pair, 128 * pair + 128)
        t1, t2 = one[:, lanes], two[:, lanes]
        heads[2 * pair] = jnp.where(mask, t1, pltpu.roll(t2, 64, 1)).astype(BF16)
        heads[2 * pair + 1] = jnp.where(mask, pltpu.roll(t1, 64, 1), t2).astype(BF16)


def attention_kernel(ids, own, other, send, keep, kv, qg, acc):
    core = ids[0]
    keys, block = kv.shape[0], 256

    @pl.when(core == 0)
    def _():
        kv[...] = own[...]
        qg[...] = other[0:1024, :]

    @pl.when(core != 0)
    def _():
        kv[...] = other[...]
        qg[...] = own[1024:2048, :]

    low = low_lanes((keys, 128))
    zero = jnp.zeros((), BF16)
    pairs = kv[...]
    key_rows = jnp.where(low, pairs, zero)
    value_rows = jnp.where(low, zero, pairs)
    key_cols = key_rows.astype(F32).T.astype(BF16)
    value_cols = value_rows.astype(F32).T.astype(BF16)
    low_q = low_lanes((block, 128))
    scale = jnp.where(low_lanes((1, 128)), HSIZE**-0.5, 1.0).astype(F32)
    acc[...] = jnp.zeros_like(acc)

    def step(i, carry):
        rows = pl.ds(pl.multiple_of(i * block, block), block)
        qb = qg[rows, :]
        s = dot(key_rows, qb, ((1,), (1,)))
        top = jnp.max(s, axis=0, keepdims=True)
        e = jnp.exp2((s - top) * (HSIZE**-0.5 * LOG2E))
        inv = 1.0 / jnp.sum(e, axis=0, keepdims=True)
        att = e * inv
        grad = dot(value_rows, qb, ((1,), (1,)))
        delta = jnp.sum(att * grad, axis=0, keepdims=True)
        weights = att.astype(BF16)
        gs = (att * (grad - delta)).astype(BF16)
        qk = jnp.where(low_q, qb, zero)
        qv = jnp.where(low_q, zero, qb)
        acc[...] += dot(gs, qk, ((1,), (0,))) + dot(weights, qv, ((1,), (0,)))
        turned = dot(key_cols, gs, ((1,), (0,))) + dot(value_cols, weights, ((1,), (0,)))
        result = (turned.T * scale).astype(BF16)

        send[pl.ds(pl.multiple_of(keys + i * block, block), block), :] = result
        return carry

    lax.fori_loop(0, 1024 // block, step, 0)

    total = acc[...] * scale
    keep[...] = total
    send[0:keys, :] = jnp.where(core == 0, 0.0, total).astype(BF16)


def merge_kernel(ids, keep, send, recv, moved, columns):
    core = ids[0]
    keys = keep.shape[0]
    half = keys // 2
    kv = (keep[...] + recv[0:keys, :].astype(F32)).astype(BF16)
    own, oth = send[keys:, :], recv[keys:, :]
    low = jnp.where(core == 0, own, oth)
    high = jnp.where(core == 0, oth, own)
    columns[:, 0:128] = kv
    columns[0:half, 128:256] = low
    columns[half:keys, 128:256] = high
    moved[0:half, :] = jnp.where(core == 0, kv[0:half], low)
    moved[half:keys, :] = jnp.where(core == 0, kv[half:keys], high)


def unpack(heads):
    mask = low_lanes((256, 128))
    one, two = [], []
    for pair in range(4):
        a, b = heads[2 * pair].astype(F32), heads[2 * pair + 1].astype(F32)
        one.append(jnp.where(mask, a, pltpu.roll(b, 64, 1)).astype(BF16))
        two.append(jnp.where(mask, pltpu.roll(a, 64, 1), b).astype(BF16))
    return jnp.concatenate(one, axis=1), jnp.concatenate(two, axis=1)


def outer_kernel(ids, columns, x0, r1, l1, r2, l2, r3, l3, r4, l4, keep, send, acc):
    core, place = ids[0], ids[2]

    def term(step, rows):
        start = lax.rem(place + step, 8) * 256
        chunk = columns[pl.ds(pl.multiple_of(start, 256), 256), :]
        return dot(rows, chunk, ((0,), (0,)))

    acc[...] = term(0, x0[...]) + term(7, r1[...]) + term(1, l1[...])
    acc[...] += term(6, r2[...]) + term(2, l2[...])
    acc[...] += term(5, r3[...]) + term(3, l3[...])
    acc[...] += term(4, jnp.concatenate([r4[...], l4[...]], axis=0))
    lane = lax.broadcasted_iota(jnp.int32, (32, 256), 1)
    mine = (lane < 192) == (core == 0)
    for part in range(4):
        for piece in range(4):
            for half in range(2):
                start = part * 256 + half * 128 + piece * 32
                value = jnp.where(mine, acc[start : start + 32, :], 0.0).astype(BF16)

                @pl.when(core == half)
                def _():
                    keep[4 * piece + part] = value

                @pl.when(core != half)
                def _():
                    send[4 * piece + part] = value


def back_kernel(ids, heads, w0t, w0b, w1t, w1b, w2t, w2b, w3t, w3b, keep, send):
    core = ids[0]
    one, two = unpack(heads)
    for step, piece in enumerate(((w0t, w0b), (w1t, w1b), (w2t, w2b), (w3t, w3b))):
        cols = pl.ds(block_of(ids, step), 256)
        weight = whole_weight(piece)
        a = dot(one, weight[:, :512], ((1,), (1,)))
        b = dot(two, weight[:, 512:], ((1,), (1,)))
        total = jnp.where(core == 0, a + b, a)
        extra = jnp.where(core == 0, 0.0, b)
        keep[0, :, cols] = jnp.where(core == 0, total[:128], total[128:])
        keep[1, :, cols] = jnp.where(core == 0, extra[:128], extra[128:])
        send[0, :, cols] = jnp.where(core == 0, total[128:], total[:128])
        send[1, :, cols] = jnp.where(core == 0, extra[128:], extra[:128])


def spread_kernel(ids, own, oth, gq, gk, gv, go):
    core = ids[0]
    mask = low_lanes((32, 128))
    scale = 32768**-0.5
    for half in range(2):
        for piece in range(4):
            rows = slice(half * 128 + piece * 32, half * 128 + piece * 32 + 32)
            for pair in range(4):
                a, b = (
                    jnp.where(core == half, own[piece, h], oth[piece, h]).astype(F32) * scale
                    for h in (2 * pair, 2 * pair + 1)
                )
                lanes = slice(128 * pair, 128 * pair + 128)
                for base, (low, high) in ((0, (gk, gv)), (128, (gq, go))):
                    ta, tb = a[:, base : base + 128], b[:, base : base + 128]
                    low[rows, lanes] = jnp.where(mask, ta, pltpu.roll(tb, 64, 1))
                    high[rows, lanes] = jnp.where(mask, pltpu.roll(ta, 64, 1), tb)


def finish_kernel(ids, sig, up, keep, recv, out, grad):
    normed_f, inverse = normalize(sig[...])
    out[...] = (sig[...].astype(F32) + keep[1] + recv[1]).astype(BF16)
    gn = keep[0] + recv[0]
    mean = jnp.mean(gn, axis=-1, keepdims=True)
    along = jnp.mean(gn * normed_f, axis=-1, keepdims=True)
    grad[...] = (up[...].astype(F32) + inverse * (gn - mean - normed_f * along)).astype(BF16)


def exchange(value, axis):
    return lax.all_to_all(value, axis, split_axis=0, concat_axis=0, tiled=True)


def body(signal, w_query, w_key, w_value, w_output, upstream):
    core, place = lax.axis_index("core"), lax.axis_index("fsdp")
    ids = jnp.stack([core, place, lax.axis_index("z")]).astype(jnp.int32)
    sig, up = signal[0], upstream[0]
    w0 = jnp.concatenate(
        [jnp.where(core == 0, w_key, w_query), jnp.where(core == 0, w_value, w_output)], axis=1
    )
    w0t, w0b = w0[:128], w0[128:]
    w1t, w3b = shift(w0t, "fsdp", 4, -1), shift(w0b, "fsdp", 4, 1)
    w1b, w3t = shift(w0b, "fsdp", 4, -1), shift(w0t, "fsdp", 4, 1)
    (own,) = call(stack_kernel, ids, [sig, up], [((2, 128, 1024), BF16)])
    oth = pair(own)
    w2t, w2b = shift(w1t, "fsdp", 4, -1), shift(w3b, "fsdp", 4, 1)
    weights = [w0t, w0b, w1t, w1b, w2t, w2b, w3t, w3b]
    x0 = jnp.concatenate(
        [
            jnp.where(core == 0, own[0], oth[1]),
            jnp.where(core == 0, oth[0], own[1]),
        ],
        axis=0,
    )
    r1, l1 = shift(x0, "z", 8, 1), shift(x0, "z", 8, -1)
    r2, l2 = shift(r1, "z", 8, 1), shift(l1, "z", 8, -1)
    r3, l3 = shift(r2, "z", 8, 1), shift(l2, "z", 8, -1)
    r4, l4 = shift(r3[:128], "z", 8, 1), shift(l3[128:], "z", 8, -1)
    heads, _, _ = call(
        project_kernel,
        ids,
        [own, oth] + weights,
        [((8, 256, 128), BF16), ((256, 1024), BF16), ((256, 1024), BF16)],
    )
    mine = exchange(heads, "z").reshape(2048, 128)
    other = pair(mine)
    send, keep = call(
        attention_kernel,
        ids,
        [mine, other],
        [((3072, 128), BF16), ((2048, 128), F32)],
        [pltpu.VMEM((2048, 128), BF16), pltpu.VMEM((1024, 128), BF16), pltpu.VMEM((2048, 128), F32)],
    )
    recv = pair(send)
    moved, columns = call(
        merge_kernel,
        ids,
        [keep, send, recv],
        [((2048, 128), BF16), ((2048, 256), BF16)],
    )
    grads = exchange(moved.reshape(8, 256, 128), "z")
    kept, sent = call(
        back_kernel,
        ids,
        [grads] + weights,
        [((2, 128, 1024), F32), ((2, 128, 1024), F32)],
    )
    got = pair(sent)
    out, grad = call(
        finish_kernel,
        ids,
        [sig, up, kept, got],
        [((128, 1024), BF16), ((128, 1024), BF16)],
    )
    share, foreign = call(
        outer_kernel,
        ids,
        [columns, x0, r1, l1, r2, l2, r3, l3, r4, l4],
        [((16, 32, 256), BF16), ((16, 32, 256), BF16)],
        [pltpu.VMEM((1024, 256), F32)],
    )
    share = share + pair(foreign)
    total = jnp.sum(exchange(share, ("dp", "fsdp")).astype(F32), axis=0).astype(BF16)
    total = exchange(jnp.broadcast_to(total[None], (8, 32, 256)), "z")
    total = exchange(jnp.broadcast_to(total[None], (4, 8, 32, 256)), "dp")
    across = pair(total)
    shares = call(spread_kernel, ids, [total, across], [((256, 512), F32)] * 4)
    return (out[None], grad[None], *shares)


def solution(mesh):
    dp, seq, fsdp = mesh.devices.shape
    split = Mesh(mesh.devices.reshape(dp, seq // 2, 2, fsdp), ("dp", "z", "core", "fsdp"))
    frames = P(("dp", "fsdp"), ("z", "core"), None)
    rows = P("fsdp", None)

    return jax.shard_map(
        body,
        mesh=split,
        in_specs=(frames, rows, rows, rows, rows, frames),
        out_specs=(frames, frames, rows, rows, rows, rows),
        check_vma=False,
    )
```

```python
import jax
import jax.numpy as jnp
from jax import lax
from jax.experimental import pallas as pl
from jax.experimental.pallas import tpu as pltpu
from jax.sharding import Mesh
from jax.sharding import PartitionSpec as P


HSIZE = 64
LOG2E = 1.4426950408889634
F32 = jnp.float32
BF16 = jnp.bfloat16


def vmem(count):
    return [pl.BlockSpec(memory_space=pltpu.VMEM) for _ in range(count)]


def smem():
    return pl.BlockSpec(memory_space=pltpu.SMEM)


def call(kernel, ids, args, outs, scratch=(), limit=12, last=False, near=True):
    shape = jax.ShapeDtypeStruct if last else pltpu.VMEM
    if near:
        args = [pltpu.with_memory_space_constraint(a, pltpu.VMEM) for a in args]
    return pl.pallas_call(
        kernel,
        in_specs=[smem()] + vmem(len(args)),
        out_specs=vmem(len(outs)),
        out_shape=[shape(s, d) for s, d in outs],
        scratch_shapes=list(scratch),
        compiler_params=pltpu.CompilerParams(vmem_limit_bytes=limit << 20),
    )(ids, *args)


def normalize(rows):
    wide = rows.astype(F32)
    centre = wide - jnp.mean(wide, axis=-1, keepdims=True)
    variance = jnp.mean(centre * centre, axis=-1, keepdims=True)
    inverse = lax.rsqrt(variance + 1e-05)
    return centre * inverse, inverse


def dot(a, b, dims):
    return lax.dot_general(a, b, (dims, ((), ())), preferred_element_type=F32)


def low_lanes(shape):
    return lax.broadcasted_iota(jnp.int32, shape, len(shape) - 1) < HSIZE


def shift(value, axis, size, by):
    return lax.ppermute(value, axis, [(i, (i + by) % size) for i in range(size)])


def pair(value):
    return shift(value, "core", 2, 1)


def block_of(ids, step):
    return pl.multiple_of(lax.rem(ids[1] + step, 4) * 256, 256)


def stack_kernel(ids, sig, up, both):
    both[0] = normalize(sig[...])[0].astype(BF16)
    both[1] = up[...]


def whole_weight(piece):
    return jnp.concatenate([part[...] for part in piece], axis=0)


def project_kernel(ids, own, oth, w0t, w0b, w1t, w1b, w2t, w2b, w3t, w3b, heads, first, second):
    core = ids[0]
    for half, both in enumerate((own, oth)):
        at = core if half == 0 else 1 - core
        rows = pl.ds(pl.multiple_of(at * 128, 128), 128)
        first[rows, :] = both[0]
        second[rows, :] = jnp.where(core == 0, both[0], both[1])
    one = two = None
    for step, piece in enumerate(((w0t, w0b), (w1t, w1b), (w2t, w2b), (w3t, w3b))):
        cols = pl.ds(block_of(ids, step), 256)
        weight = whole_weight(piece)
        a = dot(first[:, cols], weight[:, :512], ((1,), (0,)))
        b = dot(second[:, cols], weight[:, 512:], ((1,), (0,)))
        one = a if one is None else one + a
        two = b if two is None else two + b
    mask = low_lanes((256, 128))
    for pair in range(4):
        lanes = slice(128 * pair, 128 * pair + 128)
        t1, t2 = one[:, lanes], two[:, lanes]
        heads[2 * pair] = jnp.where(mask, t1, pltpu.roll(t2, 64, 1)).astype(BF16)
        heads[2 * pair + 1] = jnp.where(mask, pltpu.roll(t1, 64, 1), t2).astype(BF16)


def attention_kernel(ids, own, other, send, keep, kv, qg, acc):
    core = ids[0]
    keys, block = kv.shape[0], 256

    @pl.when(core == 0)
    def _():
        kv[...] = own[...]
        qg[...] = other[0:1024, :]

    @pl.when(core != 0)
    def _():
        kv[...] = other[...]
        qg[...] = own[1024:2048, :]

    low = low_lanes((keys, 128))
    zero = jnp.zeros((), BF16)
    pairs = kv[...]
    key_rows = jnp.where(low, pairs, zero)
    value_rows = jnp.where(low, zero, pairs)
    key_cols = key_rows.astype(F32).T.astype(BF16)
    value_cols = value_rows.astype(F32).T.astype(BF16)
    low_q = low_lanes((block, 128))
    scale = jnp.where(low_lanes((1, 128)), HSIZE**-0.5, 1.0).astype(F32)
    acc[...] = jnp.zeros_like(acc)

    def step(i, carry):
        rows = pl.ds(pl.multiple_of(i * block, block), block)
        qb = qg[rows, :]
        s = dot(key_rows, qb, ((1,), (1,)))
        top = jnp.max(s, axis=0, keepdims=True)
        e = jnp.exp2((s - top) * (HSIZE**-0.5 * LOG2E))
        inv = 1.0 / jnp.sum(e, axis=0, keepdims=True)
        att = e * inv
        grad = dot(value_rows, qb, ((1,), (1,)))
        delta = jnp.sum(att * grad, axis=0, keepdims=True)
        weights = att.astype(BF16)
        gs = (att * (grad - delta)).astype(BF16)
        qk = jnp.where(low_q, qb, zero)
        qv = jnp.where(low_q, zero, qb)
        acc[...] += dot(gs, qk, ((1,), (0,))) + dot(weights, qv, ((1,), (0,)))
        turned = dot(key_cols, gs, ((1,), (0,))) + dot(value_cols, weights, ((1,), (0,)))
        result = (turned.T * scale).astype(BF16)

        send[pl.ds(pl.multiple_of(keys + i * block, block), block), :] = result
        return carry

    lax.fori_loop(0, 1024 // block, step, 0)

    total = acc[...] * scale
    keep[...] = total
    send[0:keys, :] = jnp.where(core == 0, 0.0, total).astype(BF16)


def merge_kernel(ids, keep, send, recv, moved, columns):
    core = ids[0]
    keys = keep.shape[0]
    half = keys // 2
    kv = (keep[...] + recv[0:keys, :].astype(F32)).astype(BF16)
    own, oth = send[keys:, :], recv[keys:, :]
    low = jnp.where(core == 0, own, oth)
    high = jnp.where(core == 0, oth, own)
    columns[:, 0:128] = kv
    columns[0:half, 128:256] = low
    columns[half:keys, 128:256] = high
    moved[0:half, :] = jnp.where(core == 0, kv[0:half], low)
    moved[half:keys, :] = jnp.where(core == 0, kv[half:keys], high)


def unpack(heads):
    mask = low_lanes((256, 128))
    one, two = [], []
    for pair in range(4):
        a, b = heads[2 * pair].astype(F32), heads[2 * pair + 1].astype(F32)
        one.append(jnp.where(mask, a, pltpu.roll(b, 64, 1)).astype(BF16))
        two.append(jnp.where(mask, pltpu.roll(a, 64, 1), b).astype(BF16))
    return jnp.concatenate(one, axis=1), jnp.concatenate(two, axis=1)


def outer_kernel(ids, columns, x0, f1, b1, f2, b2, f3, b3, f4, keep, send, acc):
    core, place = ids[0], ids[2]

    def term(step, rows):
        start = lax.rem(place + jnp.where(core == 0, 8 - step, step), 8) * 256
        chunk = columns[pl.ds(pl.multiple_of(start, 256), 256), :]
        return dot(rows, chunk, ((0,), (0,)))

    acc[...] = term(0, x0[...]) + term(1, f1[...]) + term(7, b1[...])
    acc[...] += term(2, f2[...]) + term(6, b2[...])
    acc[...] += term(3, f3[...]) + term(5, b3[...]) + term(4, f4[...])
    lane = lax.broadcasted_iota(jnp.int32, (32, 256), 1)
    mine = (lane < 192) == (core == 0)
    for part in range(4):
        for piece in range(4):
            for half in range(2):
                start = part * 256 + half * 128 + piece * 32
                value = jnp.where(mine, acc[start : start + 32, :], 0.0).astype(BF16)

                @pl.when(core == half)
                def _():
                    keep[4 * piece + part] = value

                @pl.when(core != half)
                def _():
                    send[4 * piece + part] = value


def back_kernel(ids, heads, w0t, w0b, w1t, w1b, w2t, w2b, w3t, w3b, keep, send):
    core = ids[0]
    one, two = unpack(heads)
    for step, piece in enumerate(((w0t, w0b), (w1t, w1b), (w2t, w2b), (w3t, w3b))):
        cols = pl.ds(block_of(ids, step), 256)
        weight = whole_weight(piece)
        a = dot(one, weight[:, :512], ((1,), (1,)))
        b = dot(two, weight[:, 512:], ((1,), (1,)))
        total = jnp.where(core == 0, a + b, a)
        extra = jnp.where(core == 0, 0.0, b)
        keep[0, :, cols] = jnp.where(core == 0, total[:128], total[128:])
        keep[1, :, cols] = jnp.where(core == 0, extra[:128], extra[128:])
        send[0, :, cols] = jnp.where(core == 0, total[128:], total[:128])
        send[1, :, cols] = jnp.where(core == 0, extra[128:], extra[:128])


def spread_kernel(ids, own, oth, gq, gk, gv, go):
    core, place = ids[0], ids[3]
    mask = low_lanes((32, 128))
    scale = 32768**-0.5
    for half, pieces in enumerate((own, oth)):
        base = jnp.where(core == half, 0, 128)
        for step in range(4):
            start = base + lax.rem(place + step, 4) * 32
            rows = pl.ds(pl.multiple_of(start, 32), 32)
            for duo in range(4):
                a, b = (pieces[step, h].astype(F32) * scale for h in (2 * duo, 2 * duo + 1))
                lanes = slice(128 * duo, 128 * duo + 128)
                for first, (low, high) in ((0, (gk, gv)), (128, (gq, go))):
                    ta, tb = a[:, first : first + 128], b[:, first : first + 128]
                    low[rows, lanes] = jnp.where(mask, ta, pltpu.roll(tb, 64, 1))
                    high[rows, lanes] = jnp.where(mask, pltpu.roll(ta, 64, 1), tb)


def finish_kernel(ids, sig, up, keep, recv, out, grad):
    normed_f, inverse = normalize(sig[...])
    out[...] = (sig[...].astype(F32) + keep[1] + recv[1]).astype(BF16)
    gn = keep[0] + recv[0]
    mean = jnp.mean(gn, axis=-1, keepdims=True)
    along = jnp.mean(gn * normed_f, axis=-1, keepdims=True)
    grad[...] = (up[...].astype(F32) + inverse * (gn - mean - normed_f * along)).astype(BF16)


def turn(value, by):
    perm = [(2 * i, 2 * ((i + by) % 8)) for i in range(8)]
    perm += [(2 * i + 1, 2 * ((i - by) % 8) + 1) for i in range(8)]
    return lax.ppermute(value, ("z", "core"), perm)


def exchange(value, axis):
    return lax.all_to_all(value, axis, split_axis=0, concat_axis=0, tiled=True)


def body(signal, w_query, w_key, w_value, w_output, upstream):
    core, place = lax.axis_index("core"), lax.axis_index("fsdp")
    ids = jnp.stack([core, place, lax.axis_index("z"), lax.axis_index("dp")]).astype(jnp.int32)
    sig, up = signal[0], upstream[0]
    w0 = jnp.concatenate(
        [jnp.where(core == 0, w_key, w_query), jnp.where(core == 0, w_value, w_output)], axis=1
    )
    w0t, w0b = w0[:128], w0[128:]
    w1t, w3b = shift(w0t, "fsdp", 4, -1), shift(w0b, "fsdp", 4, 1)
    w1b, w3t = shift(w0b, "fsdp", 4, -1), shift(w0t, "fsdp", 4, 1)
    (own,) = call(stack_kernel, ids, [sig, up], [((2, 128, 1024), BF16)])
    oth = pair(own)
    w2t, w2b = shift(w1t, "fsdp", 4, -1), shift(w3b, "fsdp", 4, 1)
    weights = [w0t, w0b, w1t, w1b, w2t, w2b, w3t, w3b]
    x0 = jnp.concatenate(
        [
            jnp.where(core == 0, own[0], oth[1]),
            jnp.where(core == 0, oth[0], own[1]),
        ],
        axis=0,
    )
    f1, b1 = turn(x0, 1), turn(x0, -1)
    f2, b2 = turn(f1, 1), turn(b1, -1)
    f3, b3 = turn(f2, 1), turn(b2, -1)
    f4 = turn(f3, 1)
    heads, _, _ = call(
        project_kernel,
        ids,
        [own, oth] + weights,
        [((8, 256, 128), BF16), ((256, 1024), BF16), ((256, 1024), BF16)],
    )
    mine = exchange(heads, "z").reshape(2048, 128)
    other = pair(mine)
    send, keep = call(
        attention_kernel,
        ids,
        [mine, other],
        [((3072, 128), BF16), ((2048, 128), F32)],
        [pltpu.VMEM((2048, 128), BF16), pltpu.VMEM((1024, 128), BF16), pltpu.VMEM((2048, 128), F32)],
        24,
    )
    recv = pair(send)
    moved, columns = call(
        merge_kernel,
        ids,
        [keep, send, recv],
        [((2048, 128), BF16), ((2048, 256), BF16)],
        last=True,
    )
    grads = exchange(moved.reshape(8, 256, 128), "z")
    kept, sent = call(
        back_kernel,
        ids,
        [grads] + weights,
        [((2, 128, 1024), F32), ((2, 128, 1024), F32)],
    )
    got = pair(sent)
    out, grad = call(
        finish_kernel,
        ids,
        [sig, up, kept, got],
        [((128, 1024), BF16), ((128, 1024), BF16)],
        last=True,
    )
    share, foreign = call(
        outer_kernel,
        ids,
        [columns, x0, f1, b1, f2, b2, f3, b3, f4],
        [((16, 32, 256), BF16), ((16, 32, 256), BF16)],
        [pltpu.VMEM((1024, 256), F32)],
        near=False,
    )
    share = share + pair(foreign)
    total = jnp.sum(exchange(share, ("dp", "fsdp")).astype(F32), axis=0).astype(BF16)
    total = exchange(jnp.broadcast_to(total[None], (8, 32, 256)), "z")
    around = [total] + [shift(total, "dp", 4, -step) for step in (1, 3, 2)]
    total = jnp.stack([around[0], around[1], around[3], around[2]])
    across = pair(total)
    shares = call(spread_kernel, ids, [total, across], [((256, 512), F32)] * 4, last=True)
    return (out[None], grad[None], *shares)


def solution(mesh):
    dp, seq, fsdp = mesh.devices.shape
    split = Mesh(mesh.devices.reshape(dp, seq // 2, 2, fsdp), ("dp", "z", "core", "fsdp"))
    frames = P(("dp", "fsdp"), ("z", "core"), None)
    rows = P("fsdp", None)

    return jax.shard_map(
        body,
        mesh=split,
        in_specs=(frames, rows, rows, rows, rows, frames),
        out_specs=(frames, frames, rows, rows, rows, rows),
        check_vma=False,
    )
```

```python
import jax
import jax.numpy as jnp
from jax import lax
from jax.experimental import pallas as pl
from jax.experimental.pallas import tpu as pltpu
from jax.sharding import Mesh
from jax.sharding import PartitionSpec as P


HSIZE = 64
LOG2E = 1.4426950408889634
F32 = jnp.float32
BF16 = jnp.bfloat16


def vmem(count):
    return [pl.BlockSpec(memory_space=pltpu.VMEM) for _ in range(count)]


def smem():
    return pl.BlockSpec(memory_space=pltpu.SMEM)


def call(kernel, ids, args, outs, scratch=(), limit=12, shape=pltpu.VMEM, far=()):
    spaces = [pltpu.VMEM] * len(args) + [pltpu.HBM] * len(far)
    args = [pltpu.with_memory_space_constraint(a, m) for a, m in zip([*args, *far], spaces)]
    return pl.pallas_call(
        kernel,
        in_specs=[smem()] + vmem(len(args)),
        out_specs=vmem(len(outs)),
        out_shape=[shape(s, d) for s, d in outs],
        scratch_shapes=list(scratch),
        compiler_params=pltpu.CompilerParams(vmem_limit_bytes=limit << 20),
    )(ids, *args)


def normalize(rows):
    wide = rows.astype(F32)
    centre = wide - jnp.mean(wide, axis=-1, keepdims=True)
    variance = jnp.mean(centre * centre, axis=-1, keepdims=True)
    inverse = lax.rsqrt(variance + 1e-05)
    return centre * inverse, inverse


def dot(a, b, dims):
    return lax.dot_general(a, b, (dims, ((), ())), preferred_element_type=F32)


def low_lanes(shape):
    return lax.broadcasted_iota(jnp.int32, shape, len(shape) - 1) < HSIZE


def shift(value, axis, size, by):
    return lax.ppermute(value, axis, [(i, (i + by) % size) for i in range(size)])


def pair(value):
    return shift(value, "core", 2, 1)


def block_of(ids, step):
    return pl.multiple_of(lax.rem(ids[1] + step, 4) * 256, 256)


def stack_kernel(ids, sig, up, both):
    both[0] = normalize(sig[...])[0].astype(BF16)
    both[1] = up[...]


def whole_weights(ids, pieces, whole):
    upper = pl.multiple_of(lax.rem(ids[3], 2) * 128, 128)
    lower = pl.multiple_of(128 - upper, 128)
    for step in range(4):
        whole[step, pl.ds(upper, 128), :] = pieces[2 * step][...]
        whole[step, pl.ds(lower, 128), :] = pieces[2 * step + 1][...]


def project_kernel(ids, own, oth, *refs):
    pieces, (heads, first, second, whole) = refs[:8], refs[8:]
    core = ids[0]
    whole_weights(ids, pieces, whole)
    for half, both in enumerate((own, oth)):
        at = core if half == 0 else 1 - core
        rows = pl.ds(pl.multiple_of(at * 128, 128), 128)
        first[rows, :] = both[0]
        second[rows, :] = jnp.where(core == 0, both[0], both[1])
    one = two = None
    for step in range(4):
        cols = pl.ds(block_of(ids, step), 256)
        a = dot(first[:, cols], whole[step, :, :512], ((1,), (0,)))
        b = dot(second[:, cols], whole[step, :, 512:], ((1,), (0,)))
        one = a if one is None else one + a
        two = b if two is None else two + b
    mask = low_lanes((256, 128))
    for pair in range(4):
        lanes = slice(128 * pair, 128 * pair + 128)
        t1, t2 = one[:, lanes], two[:, lanes]
        heads[2 * pair] = jnp.where(mask, t1, pltpu.roll(t2, 64, 1)).astype(BF16)
        heads[2 * pair + 1] = jnp.where(mask, pltpu.roll(t1, 64, 1), t2).astype(BF16)


def attend(kv, qg, turned_kv, acc, part, blocks):
    keys, block = kv.shape[0], 256
    low = low_lanes((keys, 128))
    zero = jnp.zeros((), BF16)
    pairs = kv[...]
    key_rows = jnp.where(low, pairs, zero)
    value_rows = jnp.where(low, zero, pairs)
    upper = lax.broadcasted_iota(jnp.int32, (128, keys), 0) < HSIZE
    columns = turned_kv[...]
    key_cols = jnp.where(upper, columns, zero)
    value_cols = jnp.where(upper, zero, columns)
    low_q = low_lanes((block, 128))
    scale = jnp.where(low_lanes((1, 128)), HSIZE**-0.5, 1.0).astype(F32)

    def step(i, carry):
        start = pl.multiple_of(i * block, block)
        qb = qg[pl.ds(start, block), :]
        s = dot(key_rows, qb, ((1,), (1,)))
        top = jnp.max(s, axis=0, keepdims=True)
        e = jnp.exp2((s - top) * (HSIZE**-0.5 * LOG2E))
        inv = 1.0 / jnp.sum(e, axis=0, keepdims=True)
        att = e * inv
        grad = dot(value_rows, qb, ((1,), (1,)))
        delta = jnp.sum(att * grad, axis=0, keepdims=True)
        weights = att.astype(BF16)
        gs = (att * (grad - delta)).astype(BF16)
        qk = jnp.where(low_q, qb, zero)
        qv = jnp.where(low_q, zero, qb)
        acc[...] += dot(gs, qk, ((1,), (0,))) + dot(weights, qv, ((1,), (0,)))
        turned = dot(key_cols, gs, ((1,), (0,))) + dot(value_cols, weights, ((1,), (0,)))
        part[pl.ds(start, block), :] = (turned.T * scale).astype(BF16)
        return carry

    lax.fori_loop(*blocks, step, 0)
    return scale


def attention_kernel(ids, own, other, send, keep, kv, qg, turned_kv, part):
    core, keys = ids[0], kv.shape[0]

    @pl.when(core == 0)
    def _():
        kv[...] = own[...]
        qg[...] = other[0:1024, :]

    @pl.when(core != 0)
    def _():
        kv[...] = other[...]
        qg[...] = own[1024:2048, :]

    turned_kv[...] = kv[...].astype(F32).T.astype(BF16)
    keep[...] = jnp.zeros_like(keep)
    scale = attend(kv, qg, turned_kv, keep, part, (0, 4))
    total = keep[...] * scale
    keep[...] = total
    send[0:keys, :] = total.astype(BF16)
    send[keys:, :] = part[...]


def merge_kernel(ids, keep, send, recv, moved, columns):
    core = ids[0]
    keys = keep.shape[0]
    half = keys // 2
    kv = (keep[...] + recv[0:keys, :].astype(F32)).astype(BF16)
    own, oth = send[keys:, :], recv[keys:, :]
    low = jnp.where(core == 0, own, oth)
    high = jnp.where(core == 0, oth, own)
    columns[:, 0:128] = kv
    columns[0:half, 128:256] = low
    columns[half:keys, 128:256] = high
    moved[0:half, :] = jnp.where(core == 0, kv[0:half], low)
    moved[half:keys, :] = jnp.where(core == 0, kv[half:keys], high)


def unpack(heads):
    mask = low_lanes((256, 128))
    one, two = [], []
    for pair in range(4):
        a, b = heads[2 * pair].astype(F32), heads[2 * pair + 1].astype(F32)
        one.append(jnp.where(mask, a, pltpu.roll(b, 64, 1)).astype(BF16))
        two.append(jnp.where(mask, pltpu.roll(a, 64, 1), b).astype(BF16))
    return jnp.concatenate(one, axis=1), jnp.concatenate(two, axis=1)


def outer_kernel(ids, columns, x0, f1, b1, f2, b2, f3, b3, f4, keep, send, acc_n, acc_u):
    core, place = ids[0], ids[2]

    def chunk(step):
        block = lax.rem(place + jnp.where(core == 0, 8 - step, step), 8)
        start = block * 256 + core * 128
        return columns[pl.ds(pl.multiple_of(start, 128), 128), :]

    for index, (low, high, a, b) in enumerate(
        ((0, 4, x0, f4), (1, 7, f1, b1), (2, 6, f2, b2), (3, 5, f3, b3))
    ):
        rows = jnp.concatenate([chunk(low), chunk(high)], axis=0)
        normed = jnp.concatenate([a[0], b[0]], axis=0)
        frames = jnp.concatenate([a[1], b[1]], axis=0)
        n, u = dot(normed, rows, ((0,), (0,))), dot(frames, rows[:, 128:], ((0,), (0,)))
        acc_n[...] = n if index == 0 else acc_n[...] + n
        acc_u[...] = u if index == 0 else acc_u[...] + u
    mask = low_lanes((128, 128))
    for step in range(4):
        base = block_of(ids, step)
        for half in range(2):
            rows = pl.ds(pl.multiple_of(base + half * 128, 128), 128)
            upper = jnp.where(mask, acc_n[rows, 128:], acc_u[rows, :])
            value = jnp.concatenate([acc_n[rows, :128], upper], axis=1)

            @pl.when(core == half)
            def _():
                keep[step] = value

            @pl.when(core != half)
            def _():
                send[step] = value.astype(BF16)


def back_kernel(ids, heads, *refs):
    pieces, (keep, send, whole) = refs[:8], refs[8:]
    core = ids[0]
    one, two = unpack(heads)
    whole_weights(ids, pieces, whole)
    for step in range(4):
        cols = pl.ds(block_of(ids, step), 256)
        a = dot(one, whole[step, :, :512], ((1,), (1,)))
        b = dot(two, whole[step, :, 512:], ((1,), (1,)))
        total = jnp.where(core == 0, a + b, a)
        extra = jnp.where(core == 0, 0.0, b)
        keep[0, :, cols] = jnp.where(core == 0, total[:128], total[128:])
        keep[1, :, cols] = jnp.where(core == 0, extra[:128], extra[128:])
        send[0, :, cols] = jnp.where(core == 0, total[128:], total[:128])
        send[1, :, cols] = jnp.where(core == 0, extra[128:], extra[:128])


def spread_kernel(ids, own, oth, gq, gk, gv, go):
    core = ids[0]
    mask = low_lanes((128, 128))
    scale = 32768**-0.5
    for half, pieces in enumerate((own, oth)):
        start = jnp.where(core == half, 0, 128)
        rows = pl.ds(pl.multiple_of(start, 128), 128)
        for duo in range(4):
            a, b = (pieces[h].astype(F32) * scale for h in (2 * duo, 2 * duo + 1))
            lanes = slice(128 * duo, 128 * duo + 128)
            for first, (low, high) in ((0, (gk, gv)), (128, (gq, go))):
                ta, tb = a[:, first : first + 128], b[:, first : first + 128]
                low[rows, lanes] = jnp.where(mask, ta, pltpu.roll(tb, 64, 1))
                high[rows, lanes] = jnp.where(mask, pltpu.roll(ta, 64, 1), tb)


def finish_kernel(ids, sig, up, keep, recv, out, grad):
    normed_f, inverse = normalize(sig[...])
    out[...] = (sig[...].astype(F32) + keep[1] + recv[1]).astype(BF16)
    gn = keep[0] + recv[0]
    mean = jnp.mean(gn, axis=-1, keepdims=True)
    along = jnp.mean(gn * normed_f, axis=-1, keepdims=True)
    grad[...] = (up[...].astype(F32) + inverse * (gn - mean - normed_f * along)).astype(BF16)


def turn(value, by):
    perm = [(2 * i, 2 * ((i + by) % 8)) for i in range(8)]
    perm += [(2 * i + 1, 2 * ((i - by) % 8) + 1) for i in range(8)]
    return lax.ppermute(value, ("z", "core"), perm)


def exchange(value, axis):
    return lax.all_to_all(value, axis, split_axis=0, concat_axis=0, tiled=True)


def body(signal, w_query, w_key, w_value, w_output, upstream):
    core, place = lax.axis_index("core"), lax.axis_index("fsdp")
    ids = jnp.stack([core, place, lax.axis_index("z"), lax.axis_index("dp")]).astype(jnp.int32)
    sig, up = signal[0], upstream[0]
    w0 = jnp.concatenate(
        [jnp.where(core == 0, w_key, w_query), jnp.where(core == 0, w_value, w_output)], axis=1
    )
    even = lax.rem(lax.axis_index("dp"), 2) == 0
    w0a = jnp.where(even, w0[:128], w0[128:])
    w0b = jnp.where(even, w0[128:], w0[:128])
    w1a, w3b = shift(w0a, "fsdp", 4, -1), shift(w0b, "fsdp", 4, 1)
    (own,) = call(stack_kernel, ids, [sig, up], [((2, 128, 1024), BF16)])
    oth = pair(own)
    w2a, w1b = shift(w1a, "fsdp", 4, -1), shift(w1a, "dp", 4, -1)
    w2b, w3a = shift(w3b, "fsdp", 4, 1), shift(w3b, "dp", 4, 1)
    weights = [w0a, w0b, w1a, w1b, w2a, w2b, w3a, w3b]
    f1, b1 = turn(own, 1), turn(own, -1)
    f2, b2 = turn(f1, 1), turn(b1, -1)
    f3, b3 = turn(f2, 1), turn(b2, -1)
    f4 = turn(f3, 1)
    heads, _, _ = call(
        project_kernel,
        ids,
        [own, oth] + weights,
        [((8, 256, 128), BF16), ((256, 1024), BF16), ((256, 1024), BF16)],
        [pltpu.VMEM((4, 256, 1024), BF16)],
    )
    mine = exchange(heads, "z").reshape(2048, 128)
    other = pair(mine)
    send, keep = call(
        attention_kernel,
        ids,
        [mine, other],
        [((3072, 128), BF16), ((2048, 128), F32)],
        [
            pltpu.VMEM((2048, 128), BF16),
            pltpu.VMEM((1024, 128), BF16),
            pltpu.VMEM((128, 2048), BF16),
            pltpu.VMEM((1024, 128), BF16),
        ],
        24,
    )
    recv = pair(send)
    moved, columns = call(
        merge_kernel,
        ids,
        [keep, send, recv],
        [((2048, 128), BF16), ((2048, 256), BF16)],
        shape=pltpu.HBM,
    )
    grads = exchange(moved.reshape(8, 256, 128), "z")
    kept, sent = call(
        back_kernel,
        ids,
        [grads],
        [((2, 128, 1024), F32), ((2, 128, 1024), F32)],
        [pltpu.VMEM((4, 256, 1024), BF16)],
        far=weights,
    )
    got = pair(sent)
    out, grad = call(
        finish_kernel,
        ids,
        [sig, up, kept, got],
        [((128, 1024), BF16), ((128, 1024), BF16)],
        shape=pltpu.HBM,
    )
    share, foreign = call(
        outer_kernel,
        ids,
        [],
        [((4, 128, 256), F32), ((4, 128, 256), BF16)],
        [pltpu.VMEM((1024, 256), F32), pltpu.VMEM((1024, 128), F32)],
        far=[columns, own, f1, b1, f2, b2, f3, b3, f4],
    )
    foreign = pair(foreign)
    share = [(share[i] + foreign[i].astype(F32)).astype(BF16) for i in range(4)]
    total = share[0].astype(F32)
    for step in (1, 3, 2):
        total += shift(share[step], "fsdp", 4, step).astype(F32)
    mine = total.astype(BF16)
    total = mine.astype(F32)
    for step in (1, 3, 2):
        total += shift(mine, "dp", 4, step).astype(F32)
    total = exchange(jnp.broadcast_to(total.astype(BF16)[None], (8, 128, 256)), "z")
    across = pair(total)
    shares = call(spread_kernel, ids, [total, across], [((256, 512), F32)] * 4, shape=pltpu.HBM)
    return (out[None], grad[None], *shares)


def solution(mesh):
    dp, seq, fsdp = mesh.devices.shape
    split = Mesh(mesh.devices.reshape(dp, seq // 2, 2, fsdp), ("dp", "z", "core", "fsdp"))
    frames = P(("dp", "fsdp"), ("z", "core"), None)
    rows = P("fsdp", None)

    return jax.shard_map(
        body,
        mesh=split,
        in_specs=(frames, rows, rows, rows, rows, frames),
        out_specs=(frames, frames, rows, rows, rows, rows),
        check_vma=False,
    )
```

```python
import jax
import jax.numpy as jnp
from jax import lax
from jax.experimental import pallas as pl
from jax.experimental.pallas import tpu as pltpu
from jax.sharding import Mesh
from jax.sharding import PartitionSpec as P


HSIZE = 64
LOG2E = 1.4426950408889634
F32 = jnp.float32
BF16 = jnp.bfloat16


def vmem(count):
    return [pl.BlockSpec(memory_space=pltpu.VMEM) for _ in range(count)]


def smem():
    return pl.BlockSpec(memory_space=pltpu.SMEM)


def call(kernel, ids, args, outs, scratch=(), limit=12, shape=pltpu.VMEM, far=()):
    spaces = [pltpu.VMEM] * len(args) + [pltpu.HBM] * len(far)
    args = [pltpu.with_memory_space_constraint(a, m) for a, m in zip([*args, *far], spaces)]
    return pl.pallas_call(
        kernel,
        in_specs=[smem()] + vmem(len(args)),
        out_specs=vmem(len(outs)),
        out_shape=[shape(s, d) for s, d in outs],
        scratch_shapes=list(scratch),
        compiler_params=pltpu.CompilerParams(vmem_limit_bytes=limit << 20),
    )(ids, *args)


def normalize(rows):
    wide = rows.astype(F32)
    centre = wide - jnp.mean(wide, axis=-1, keepdims=True)
    variance = jnp.mean(centre * centre, axis=-1, keepdims=True)
    inverse = lax.rsqrt(variance + 1e-05)
    return centre * inverse, inverse


def dot(a, b, dims):
    return lax.dot_general(a, b, (dims, ((), ())), preferred_element_type=F32)


def low_lanes(shape):
    return lax.broadcasted_iota(jnp.int32, shape, len(shape) - 1) < HSIZE


def shift(value, axis, size, by):
    return lax.ppermute(value, axis, [(i, (i + by) % size) for i in range(size)])


def pair(value):
    return shift(value, "core", 2, 1)


def block_of(ids, step):
    return pl.multiple_of(lax.rem(ids[1] + step, 4) * 256, 256)


def stack_kernel(ids, sig, up, both):
    both[0] = normalize(sig[...])[0].astype(BF16)
    both[1] = up[...]


def whole_weights(ids, pieces, whole):
    upper = pl.multiple_of(lax.rem(ids[3], 2) * 128, 128)
    lower = pl.multiple_of(128 - upper, 128)
    for step in range(4):
        whole[step, pl.ds(upper, 128), :] = pieces[2 * step][...]
        whole[step, pl.ds(lower, 128), :] = pieces[2 * step + 1][...]


def project_kernel(ids, own, oth, *refs):
    pieces, (heads, first, second, whole) = refs[:8], refs[8:]
    core = ids[0]
    whole_weights(ids, pieces, whole)
    for half, both in enumerate((own, oth)):
        at = core if half == 0 else 1 - core
        rows = pl.ds(pl.multiple_of(at * 128, 128), 128)
        first[rows, :] = both[0]
        second[rows, :] = jnp.where(core == 0, both[0], both[1])
    one = two = None
    for step in range(4):
        cols = pl.ds(block_of(ids, step), 256)
        a = dot(first[:, cols], whole[step, :, :512], ((1,), (0,)))
        b = dot(second[:, cols], whole[step, :, 512:], ((1,), (0,)))
        one = a if one is None else one + a
        two = b if two is None else two + b
    mask = low_lanes((256, 128))
    for pair in range(4):
        lanes = slice(128 * pair, 128 * pair + 128)
        t1, t2 = one[:, lanes], two[:, lanes]
        heads[2 * pair] = jnp.where(mask, t1, pltpu.roll(t2, 64, 1)).astype(BF16)
        heads[2 * pair + 1] = jnp.where(mask, pltpu.roll(t1, 64, 1), t2).astype(BF16)


def attend(kv, qg, turned_kv, acc, part, blocks):
    keys, block = kv.shape[0], 512
    low = low_lanes((keys, 128))
    zero = jnp.zeros((), BF16)
    pairs = kv[...]
    key_rows = jnp.where(low, pairs, zero)
    value_rows = jnp.where(low, zero, pairs)
    upper = lax.broadcasted_iota(jnp.int32, (128, keys), 0) < HSIZE
    columns = turned_kv[...]
    key_cols = jnp.where(upper, columns, zero)
    value_cols = jnp.where(upper, zero, columns)
    low_q = low_lanes((block, 128))
    scale = jnp.where(low_lanes((1, 128)), HSIZE**-0.5, 1.0).astype(F32)

    def step(i, carry):
        start = pl.multiple_of(i * block, block)
        qb = qg[pl.ds(start, block), :]
        s = dot(key_rows, qb, ((1,), (1,)))
        top = jnp.max(s, axis=0, keepdims=True)
        e = jnp.exp2((s - top) * (HSIZE**-0.5 * LOG2E))
        inv = 1.0 / jnp.sum(e, axis=0, keepdims=True)
        att = e * inv
        grad = dot(value_rows, qb, ((1,), (1,)))
        delta = jnp.sum(att * grad, axis=0, keepdims=True)
        weights = att.astype(BF16)
        gs = (att * (grad - delta)).astype(BF16)
        qk = jnp.where(low_q, qb, zero)
        qv = jnp.where(low_q, zero, qb)
        both, queries = jnp.concatenate([gs, weights], axis=1), jnp.concatenate([qk, qv], axis=0)
        acc[...] += dot(both, queries, ((1,), (0,)))
        turned = dot(key_cols, gs, ((1,), (0,))) + dot(value_cols, weights, ((1,), (0,)))
        part[pl.ds(start, block), :] = (turned.T * scale).astype(BF16)
        return carry

    lax.fori_loop(*blocks, step, 0)
    return scale


def attention_kernel(ids, own, other, send, keep, kv, qg, turned_kv, part):
    core, keys = ids[0], kv.shape[0]

    @pl.when(core == 0)
    def _():
        kv[...] = own[...]
        qg[...] = other[0:1024, :]

    @pl.when(core != 0)
    def _():
        kv[...] = other[...]
        qg[...] = own[1024:2048, :]

    turned_kv[...] = kv[...].astype(F32).T.astype(BF16)
    keep[...] = jnp.zeros_like(keep)
    scale = attend(kv, qg, turned_kv, keep, part, (0, 2))
    total = keep[...] * scale
    keep[...] = total
    send[0:keys, :] = total.astype(BF16)
    send[keys:, :] = part[...]


def merge_kernel(ids, keep, send, recv, moved, columns):
    core = ids[0]
    keys = keep.shape[0]
    half = keys // 2
    kv = (keep[...] + recv[0:keys, :].astype(F32)).astype(BF16)
    own, oth = send[keys:, :], recv[keys:, :]
    low = jnp.where(core == 0, own, oth)
    high = jnp.where(core == 0, oth, own)
    columns[:, 0:128] = kv
    columns[0:half, 128:256] = low
    columns[half:keys, 128:256] = high
    moved[0:half, :] = jnp.where(core == 0, kv[0:half], low)
    moved[half:keys, :] = jnp.where(core == 0, kv[half:keys], high)


def unpack(heads):
    mask = low_lanes((256, 128))
    one, two = [], []
    for pair in range(4):
        a, b = heads[2 * pair].astype(F32), heads[2 * pair + 1].astype(F32)
        one.append(jnp.where(mask, a, pltpu.roll(b, 64, 1)).astype(BF16))
        two.append(jnp.where(mask, pltpu.roll(a, 64, 1), b).astype(BF16))
    return jnp.concatenate(one, axis=1), jnp.concatenate(two, axis=1)


def outer_kernel(ids, columns, x0, f1, b1, f2, b2, f3, b3, f4, keep, send, acc_n, acc_u):
    core, place = ids[0], ids[2]

    def chunk(step):
        block = lax.rem(place + jnp.where(core == 0, 8 - step, step), 8)
        start = block * 256 + core * 128
        return columns[pl.ds(pl.multiple_of(start, 128), 128), :]

    for index, (low, high, a, b) in enumerate(
        ((0, 4, x0, f4), (1, 7, f1, b1), (2, 6, f2, b2), (3, 5, f3, b3))
    ):
        rows = jnp.concatenate([chunk(low), chunk(high)], axis=0)
        normed = jnp.concatenate([a[0], b[0]], axis=0)
        frames = jnp.concatenate([a[1], b[1]], axis=0)
        n, u = dot(normed, rows, ((0,), (0,))), dot(frames, rows[:, 128:], ((0,), (0,)))
        acc_n[...] = n if index == 0 else acc_n[...] + n
        acc_u[...] = u if index == 0 else acc_u[...] + u
    mask = low_lanes((128, 128))
    for step in range(4):
        base = block_of(ids, step)
        for half in range(2):
            rows = pl.ds(pl.multiple_of(base + half * 128, 128), 128)
            upper = jnp.where(mask, acc_n[rows, 128:], acc_u[rows, :])
            value = jnp.concatenate([acc_n[rows, :128], upper], axis=1)

            @pl.when(core == half)
            def _():
                keep[step] = value

            @pl.when(core != half)
            def _():
                send[step] = value.astype(BF16)


def back_kernel(ids, heads, *refs):
    pieces, (keep, send, whole) = refs[:8], refs[8:]
    core = ids[0]
    one, two = unpack(heads)
    whole_weights(ids, pieces, whole)
    for step in range(4):
        cols = pl.ds(block_of(ids, step), 256)
        a = dot(one, whole[step, :, :512], ((1,), (1,)))
        b = dot(two, whole[step, :, 512:], ((1,), (1,)))
        total = jnp.where(core == 0, a + b, a)
        extra = jnp.where(core == 0, 0.0, b)
        keep[0, :, cols] = jnp.where(core == 0, total[:128], total[128:])
        keep[1, :, cols] = jnp.where(core == 0, extra[:128], extra[128:])
        send[0, :, cols] = jnp.where(core == 0, total[128:], total[:128])
        send[1, :, cols] = jnp.where(core == 0, extra[128:], extra[:128])


NEAR, FAR = (0, 1, 7, 2, 6), (3, 4, 5)


def spread_kernel(ids, *refs):
    own, (near, far), (gq, gk, gv, go, heads) = refs[:8], refs[8:10], refs[10:]
    oth = {step: near.at[i] for i, step in enumerate(NEAR)}
    oth.update({step: far.at[i] for i, step in enumerate(FAR)})
    core, place = ids[0], ids[2]
    mask = low_lanes((128, 128))
    scale = 32768**-0.5
    for half, pieces in enumerate((own, oth)):
        for step in range(8):
            back = core if half == 1 else 1 - core
            heads[lax.rem(place + jnp.where(back == 1, 8 - step, step), 8)] = pieces[step][...]
        start = jnp.where(core == half, 0, 128)
        rows = pl.ds(pl.multiple_of(start, 128), 128)
        for duo in range(4):
            a, b = (heads[h].astype(F32) * scale for h in (2 * duo, 2 * duo + 1))
            lanes = slice(128 * duo, 128 * duo + 128)
            for first, (low, high) in ((0, (gk, gv)), (128, (gq, go))):
                ta, tb = a[:, first : first + 128], b[:, first : first + 128]
                low[rows, lanes] = jnp.where(mask, ta, pltpu.roll(tb, 64, 1))
                high[rows, lanes] = jnp.where(mask, pltpu.roll(ta, 64, 1), tb)


def finish_kernel(ids, sig, up, keep, recv, out, grad):
    normed_f, inverse = normalize(sig[...])
    out[...] = (sig[...].astype(F32) + keep[1] + recv[1]).astype(BF16)
    gn = keep[0] + recv[0]
    mean = jnp.mean(gn, axis=-1, keepdims=True)
    along = jnp.mean(gn * normed_f, axis=-1, keepdims=True)
    grad[...] = (up[...].astype(F32) + inverse * (gn - mean - normed_f * along)).astype(BF16)


def turn(value, by):
    perm = [(2 * i, 2 * ((i + by) % 8)) for i in range(8)]
    perm += [(2 * i + 1, 2 * ((i - by) % 8) + 1) for i in range(8)]
    return lax.ppermute(value, ("z", "core"), perm)


def exchange(value, axis):
    return lax.all_to_all(value, axis, split_axis=0, concat_axis=0, tiled=True)


def body(signal, w_query, w_key, w_value, w_output, upstream):
    core, place = lax.axis_index("core"), lax.axis_index("fsdp")
    ids = jnp.stack([core, place, lax.axis_index("z"), lax.axis_index("dp")]).astype(jnp.int32)
    sig, up = signal[0], upstream[0]
    w0 = jnp.concatenate(
        [jnp.where(core == 0, w_key, w_query), jnp.where(core == 0, w_value, w_output)], axis=1
    )
    even = lax.rem(lax.axis_index("dp"), 2) == 0
    w0a = jnp.where(even, w0[:128], w0[128:])
    w0b = jnp.where(even, w0[128:], w0[:128])
    w1a, w3b = shift(w0a, "fsdp", 4, -1), shift(w0b, "fsdp", 4, 1)
    (own,) = call(stack_kernel, ids, [sig, up], [((2, 128, 1024), BF16)])
    oth = pair(own)
    w2a, w1b = shift(w1a, "fsdp", 4, -1), shift(w1a, "dp", 4, -1)
    w2b, w3a = shift(w3b, "fsdp", 4, 1), shift(w3b, "dp", 4, 1)
    weights = [w0a, w0b, w1a, w1b, w2a, w2b, w3a, w3b]
    f1, b1 = turn(own, 1), turn(own, -1)
    f2, b2 = turn(f1, 1), turn(b1, -1)
    f3, b3 = turn(f2, 1), turn(b2, -1)
    f4 = turn(f3, 1)
    heads, _, _ = call(
        project_kernel,
        ids,
        [own, oth] + weights,
        [((8, 256, 128), BF16), ((256, 1024), BF16), ((256, 1024), BF16)],
        [pltpu.VMEM((4, 256, 1024), BF16)],
    )
    mine = exchange(heads, "z").reshape(2048, 128)
    other = pair(mine)
    send, keep = call(
        attention_kernel,
        ids,
        [mine, other],
        [((3072, 128), BF16), ((2048, 128), F32)],
        [
            pltpu.VMEM((2048, 128), BF16),
            pltpu.VMEM((1024, 128), BF16),
            pltpu.VMEM((128, 2048), BF16),
            pltpu.VMEM((1024, 128), BF16),
        ],
        30,
    )
    recv = pair(send)
    moved, columns = call(
        merge_kernel,
        ids,
        [keep, send, recv],
        [((2048, 128), BF16), ((2048, 256), BF16)],
        shape=pltpu.HBM,
    )
    grads = exchange(moved.reshape(8, 256, 128), "z")
    kept, sent = call(
        back_kernel,
        ids,
        [grads],
        [((2, 128, 1024), F32), ((2, 128, 1024), F32)],
        [pltpu.VMEM((4, 256, 1024), BF16)],
        far=weights,
    )
    got = pair(sent)
    out, grad = call(
        finish_kernel,
        ids,
        [sig, up, kept, got],
        [((128, 1024), BF16), ((128, 1024), BF16)],
        shape=pltpu.HBM,
    )
    share, foreign = call(
        outer_kernel,
        ids,
        [],
        [((4, 128, 256), F32), ((4, 128, 256), BF16)],
        [pltpu.VMEM((1024, 256), F32), pltpu.VMEM((1024, 128), F32)],
        far=[columns, own, f1, b1, f2, b2, f3, b3, f4],
    )
    foreign = pair(foreign)
    share = [(share[i] + foreign[i].astype(F32)).astype(BF16) for i in range(4)]
    total = share[0].astype(F32)
    for step in (1, 3, 2):
        total += shift(share[step], "fsdp", 4, step).astype(F32)
    mine = total.astype(BF16)
    total = mine.astype(F32)
    for step in (1, 3, 2):
        total += shift(mine, "dp", 4, step).astype(F32)
    total = total.astype(BF16)
    p2, p6 = turn(total, 2), turn(total, -2)
    p1, p7 = turn(total, 1), turn(total, -1)
    p3, p4, p5 = turn(p2, 1), turn(p2, 2), turn(p6, -1)
    pieces = [total, p1, p2, p3, p4, p5, p6, p7]
    across = [pair(jnp.stack([pieces[i] for i in NEAR])), pair(jnp.stack([pieces[i] for i in FAR]))]
    shares = call(
        spread_kernel,
        ids,
        pieces + across,
        [((256, 512), F32)] * 4,
        [pltpu.VMEM((8, 128, 256), BF16)],
        shape=pltpu.HBM,
    )
    return (out[None], grad[None], *shares)


def solution(mesh):
    dp, seq, fsdp = mesh.devices.shape
    split = Mesh(mesh.devices.reshape(dp, seq // 2, 2, fsdp), ("dp", "z", "core", "fsdp"))
    frames = P(("dp", "fsdp"), ("z", "core"), None)
    rows = P("fsdp", None)

    return jax.shard_map(
        body,
        mesh=split,
        in_specs=(frames, rows, rows, rows, rows, frames),
        out_specs=(frames, frames, rows, rows, rows, rows),
        check_vma=False,
    )
```

```python
import jax
import jax.numpy as jnp
from jax import lax
from jax.experimental import pallas as pl
from jax.experimental.pallas import tpu as pltpu
from jax.sharding import Mesh
from jax.sharding import PartitionSpec as P


HSIZE = 64
LOG2E = 1.4426950408889634
F32 = jnp.float32
BF16 = jnp.bfloat16


def vmem(count):
    return [pl.BlockSpec(memory_space=pltpu.VMEM) for _ in range(count)]


def smem():
    return pl.BlockSpec(memory_space=pltpu.SMEM)


def call(kernel, ids, args, outs, scratch=(), limit=12, shape=pltpu.VMEM, far=()):
    spaces = [pltpu.VMEM] * len(args) + [pltpu.HBM] * len(far)
    args = [pltpu.with_memory_space_constraint(a, m) for a, m in zip([*args, *far], spaces)]
    return pl.pallas_call(
        kernel,
        in_specs=[smem()] + vmem(len(args)),
        out_specs=vmem(len(outs)),
        out_shape=[shape(s, d) for s, d in outs],
        scratch_shapes=list(scratch),
        compiler_params=pltpu.CompilerParams(vmem_limit_bytes=limit << 20),
    )(ids, *args)


def normalize(rows):
    wide = rows.astype(F32)
    centre = wide - jnp.mean(wide, axis=-1, keepdims=True)
    variance = jnp.mean(centre * centre, axis=-1, keepdims=True)
    inverse = lax.rsqrt(variance + 1e-05)
    return centre * inverse, inverse


def dot(a, b, dims):
    return lax.dot_general(a, b, (dims, ((), ())), preferred_element_type=F32)


def low_lanes(shape):
    return lax.broadcasted_iota(jnp.int32, shape, len(shape) - 1) < HSIZE


def shift(value, axis, size, by):
    return lax.ppermute(value, axis, [(i, (i + by) % size) for i in range(size)])


def pair(value):
    return shift(value, "core", 2, 1)


def block_of(ids, step):
    return pl.multiple_of(lax.rem(ids[1] + step, 4) * 256, 256)


def stack_kernel(ids, sig, up, both):
    both[0] = normalize(sig[...])[0].astype(BF16)
    both[1] = up[...]


def whole_weights(ids, pieces, whole):
    upper = pl.multiple_of(lax.rem(ids[3], 2) * 128, 128)
    lower = pl.multiple_of(128 - upper, 128)
    for step in range(4):
        whole[step, pl.ds(upper, 128), :] = pieces[2 * step][...]
        whole[step, pl.ds(lower, 128), :] = pieces[2 * step + 1][...]


def project_kernel(ids, own, oth, *refs):
    pieces, (heads, first, second, whole) = refs[:8], refs[8:]
    core = ids[0]
    whole_weights(ids, pieces, whole)
    for half, both in enumerate((own, oth)):
        at = core if half == 0 else 1 - core
        rows = pl.ds(pl.multiple_of(at * 128, 128), 128)
        first[rows, :] = both[0]
        second[rows, :] = jnp.where(core == 0, both[0], both[1])
    one = two = None
    for step in range(4):
        cols = pl.ds(block_of(ids, step), 256)
        a = dot(first[:, cols], whole[step, :, :512], ((1,), (0,)))
        b = dot(second[:, cols], whole[step, :, 512:], ((1,), (0,)))
        one = a if one is None else one + a
        two = b if two is None else two + b
    mask = low_lanes((256, 128))
    for pair in range(4):
        lanes = slice(128 * pair, 128 * pair + 128)
        t1, t2 = one[:, lanes], two[:, lanes]
        heads[2 * pair] = jnp.where(mask, t1, pltpu.roll(t2, 64, 1)).astype(BF16)
        heads[2 * pair + 1] = jnp.where(mask, pltpu.roll(t1, 64, 1), t2).astype(BF16)


def attend(kv, qg, turned_kv, acc, part, blocks):
    keys, block = kv.shape[0], 512
    low = low_lanes((keys, 128))
    zero = jnp.zeros((), BF16)
    pairs = kv[...]
    key_rows = jnp.where(low, pairs, zero)
    value_rows = jnp.where(low, zero, pairs)
    upper = lax.broadcasted_iota(jnp.int32, (128, keys), 0) < HSIZE
    columns = turned_kv[...]
    key_cols = jnp.where(upper, columns, zero)
    value_cols = jnp.where(upper, zero, columns)
    low_q = low_lanes((block, 128))
    scale = jnp.where(low_lanes((1, 128)), HSIZE**-0.5, 1.0).astype(F32)

    def step(i, carry):
        start = pl.multiple_of(i * block, block)
        qb = qg[pl.ds(start, block), :]
        s = dot(key_rows, qb, ((1,), (1,)))
        top = jnp.max(s, axis=0, keepdims=True)
        e = jnp.exp2((s - top) * (HSIZE**-0.5 * LOG2E))
        inv = 1.0 / jnp.sum(e, axis=0, keepdims=True)
        att = e * inv
        grad = dot(value_rows, qb, ((1,), (1,)))
        delta = jnp.sum(att * grad, axis=0, keepdims=True)
        weights = att.astype(BF16)
        gs = (att * (grad - delta)).astype(BF16)
        qk = jnp.where(low_q, qb, zero)
        qv = jnp.where(low_q, zero, qb)
        both, queries = jnp.concatenate([gs, weights], axis=1), jnp.concatenate([qk, qv], axis=0)
        acc[...] += dot(both, queries, ((1,), (0,)))
        turned = dot(key_cols, gs, ((1,), (0,))) + dot(value_cols, weights, ((1,), (0,)))
        part[pl.ds(start, block), :] = (turned.T * scale).astype(BF16)
        return carry

    lax.fori_loop(*blocks, step, 0)
    return scale


def attention_kernel(ids, own, other, send, keep, kv, qg, turned_kv, part):
    core, keys = ids[0], kv.shape[0]

    @pl.when(core == 0)
    def _():
        kv[...] = own[...]
        qg[...] = other[0:1024, :]

    @pl.when(core != 0)
    def _():
        kv[...] = other[...]
        qg[...] = own[1024:2048, :]

    turned_kv[...] = kv[...].astype(F32).T.astype(BF16)
    keep[...] = jnp.zeros_like(keep)
    scale = attend(kv, qg, turned_kv, keep, part, (0, 2))
    total = keep[...] * scale
    keep[...] = total
    send[0:keys, :] = total.astype(BF16)
    send[keys:, :] = part[...]


def merge_kernel(ids, keep, send, recv, moved, columns):
    core = ids[0]
    keys = keep.shape[0]
    half = keys // 2
    kv = (keep[...] + recv[0:keys, :].astype(F32)).astype(BF16)
    own, oth = send[keys:, :], recv[keys:, :]
    low = jnp.where(core == 0, own, oth)
    high = jnp.where(core == 0, oth, own)
    columns[:, 0:128] = kv
    columns[0:half, 128:256] = low
    columns[half:keys, 128:256] = high
    moved[0:half, :] = jnp.where(core == 0, kv[0:half], low)
    moved[half:keys, :] = jnp.where(core == 0, kv[half:keys], high)


def unpack(heads):
    mask = low_lanes((256, 128))
    one, two = [], []
    for pair in range(4):
        a, b = heads[2 * pair].astype(F32), heads[2 * pair + 1].astype(F32)
        one.append(jnp.where(mask, a, pltpu.roll(b, 64, 1)).astype(BF16))
        two.append(jnp.where(mask, pltpu.roll(a, 64, 1), b).astype(BF16))
    return jnp.concatenate(one, axis=1), jnp.concatenate(two, axis=1)


def outer_kernel(ids, b3, f4, columns, x0, f1, b1, f2, b2, f3, keep, send, acc_n, acc_u):
    core, place = ids[0], ids[2]

    def chunk(step):
        block = lax.rem(place + jnp.where(core == 0, 8 - step, step), 8)
        start = block * 256 + core * 128
        return columns[pl.ds(pl.multiple_of(start, 128), 128), :]

    for index, (low, high, a, b) in enumerate(
        ((0, 4, x0, f4), (1, 7, f1, b1), (2, 6, f2, b2), (3, 5, f3, b3))
    ):
        rows = jnp.concatenate([chunk(low), chunk(high)], axis=0)
        normed = jnp.concatenate([a[0], b[0]], axis=0)
        frames = jnp.concatenate([a[1], b[1]], axis=0)
        n, u = dot(normed, rows, ((0,), (0,))), dot(frames, rows[:, 128:], ((0,), (0,)))
        acc_n[...] = n if index == 0 else acc_n[...] + n
        acc_u[...] = u if index == 0 else acc_u[...] + u
    mask = low_lanes((128, 128))
    for step in range(4):
        base = block_of(ids, step)
        for half in range(2):
            rows = pl.ds(pl.multiple_of(base + half * 128, 128), 128)
            upper = jnp.where(mask, acc_n[rows, 128:], acc_u[rows, :])
            value = jnp.concatenate([acc_n[rows, :128], upper], axis=1)

            @pl.when(core == half)
            def _():
                keep[step] = value

            @pl.when(core != half)
            def _():
                send[step] = value.astype(BF16)


def back_kernel(ids, heads, *refs):
    pieces, (keep, send, whole) = refs[:8], refs[8:]
    core = ids[0]
    one, two = unpack(heads)
    whole_weights(ids, pieces, whole)
    for step in range(4):
        cols = pl.ds(block_of(ids, step), 256)
        a = dot(one, whole[step, :, :512], ((1,), (1,)))
        b = dot(two, whole[step, :, 512:], ((1,), (1,)))
        total = jnp.where(core == 0, a + b, a)
        extra = jnp.where(core == 0, 0.0, b)
        keep[0, :, cols] = jnp.where(core == 0, total[:128], total[128:])
        keep[1, :, cols] = jnp.where(core == 0, extra[:128], extra[128:])
        send[0, :, cols] = jnp.where(core == 0, total[128:], total[:128])
        send[1, :, cols] = jnp.where(core == 0, extra[128:], extra[:128])


NEAR, FAR = (0, 1, 7, 2, 6), (3, 4, 5)


def spread_kernel(ids, *refs):
    own, (near, far), (gq, gk, gv, go, heads) = refs[:8], refs[8:10], refs[10:]
    oth = {step: near.at[i] for i, step in enumerate(NEAR)}
    oth.update({step: far.at[i] for i, step in enumerate(FAR)})
    core, place = ids[0], ids[2]
    mask = low_lanes((128, 128))
    scale = 32768**-0.5
    for half, pieces in enumerate((own, oth)):
        for step in range(8):
            back = core if half == 1 else 1 - core
            heads[lax.rem(place + jnp.where(back == 1, 8 - step, step), 8)] = pieces[step][...]
        start = jnp.where(core == half, 0, 128)
        rows = pl.ds(pl.multiple_of(start, 128), 128)
        for duo in range(4):
            a, b = (heads[h].astype(F32) * scale for h in (2 * duo, 2 * duo + 1))
            lanes = slice(128 * duo, 128 * duo + 128)
            for first, (low, high) in ((0, (gk, gv)), (128, (gq, go))):
                ta, tb = a[:, first : first + 128], b[:, first : first + 128]
                low[rows, lanes] = jnp.where(mask, ta, pltpu.roll(tb, 64, 1))
                high[rows, lanes] = jnp.where(mask, pltpu.roll(ta, 64, 1), tb)


def finish_kernel(ids, sig, up, keep, recv, out, grad):
    normed_f, inverse = normalize(sig[...])
    out[...] = (sig[...].astype(F32) + keep[1] + recv[1]).astype(BF16)
    gn = keep[0] + recv[0]
    mean = jnp.mean(gn, axis=-1, keepdims=True)
    along = jnp.mean(gn * normed_f, axis=-1, keepdims=True)
    grad[...] = (up[...].astype(F32) + inverse * (gn - mean - normed_f * along)).astype(BF16)


def turn(value, by):
    perm = [(2 * i, 2 * ((i + by) % 8)) for i in range(8)]
    perm += [(2 * i + 1, 2 * ((i - by) % 8) + 1) for i in range(8)]
    return lax.ppermute(value, ("z", "core"), perm)


def exchange(value, axis):
    return lax.all_to_all(value, axis, split_axis=0, concat_axis=0, tiled=True)


def body(signal, w_query, w_key, w_value, w_output, upstream):
    core, place = lax.axis_index("core"), lax.axis_index("fsdp")
    ids = jnp.stack([core, place, lax.axis_index("z"), lax.axis_index("dp")]).astype(jnp.int32)
    sig, up = signal[0], upstream[0]
    w0 = jnp.concatenate(
        [jnp.where(core == 0, w_key, w_query), jnp.where(core == 0, w_value, w_output)], axis=1
    )
    even = lax.rem(lax.axis_index("dp"), 2) == 0
    w0a = jnp.where(even, w0[:128], w0[128:])
    w0b = jnp.where(even, w0[128:], w0[:128])
    w1a, w3b = shift(w0a, "fsdp", 4, -1), shift(w0b, "fsdp", 4, 1)
    (own,) = call(stack_kernel, ids, [sig, up], [((2, 128, 1024), BF16)])
    oth = pair(own)
    w2a, w1b = shift(w1a, "fsdp", 4, -1), shift(w1a, "dp", 4, -1)
    w2b, w3a = shift(w3b, "fsdp", 4, 1), shift(w3b, "dp", 4, 1)
    weights = [w0a, w0b, w1a, w1b, w2a, w2b, w3a, w3b]
    f1, b1 = turn(own, 1), turn(own, -1)
    f2, b2 = turn(f1, 1), turn(b1, -1)
    f3, b3 = turn(f2, 1), turn(b2, -1)
    f4 = turn(f3, 1)
    heads, _, _ = call(
        project_kernel,
        ids,
        [own, oth] + weights,
        [((8, 256, 128), BF16), ((256, 1024), BF16), ((256, 1024), BF16)],
        [pltpu.VMEM((4, 256, 1024), BF16)],
    )
    mine = exchange(heads, "z").reshape(2048, 128)
    other = pair(mine)
    send, keep = call(
        attention_kernel,
        ids,
        [mine, other],
        [((3072, 128), BF16), ((2048, 128), F32)],
        [
            pltpu.VMEM((2048, 128), BF16),
            pltpu.VMEM((1024, 128), BF16),
            pltpu.VMEM((128, 2048), BF16),
            pltpu.VMEM((1024, 128), BF16),
        ],
        30,
    )
    recv = pair(send)
    moved, columns = call(
        merge_kernel,
        ids,
        [keep, send, recv],
        [((2048, 128), BF16), ((2048, 256), BF16)],
        shape=pltpu.HBM,
    )
    grads = exchange(moved.reshape(8, 256, 128), "z")
    kept, sent = call(
        back_kernel,
        ids,
        [grads],
        [((2, 128, 1024), F32), ((2, 128, 1024), F32)],
        [pltpu.VMEM((4, 256, 1024), BF16)],
        far=weights,
    )
    got = pair(sent)
    out, grad = call(
        finish_kernel,
        ids,
        [sig, up, kept, got],
        [((128, 1024), BF16), ((128, 1024), BF16)],
        shape=pltpu.HBM,
    )
    share, foreign = call(
        outer_kernel,
        ids,
        [b3, f4],
        [((4, 128, 256), F32), ((4, 128, 256), BF16)],
        [pltpu.VMEM((1024, 256), F32), pltpu.VMEM((1024, 128), F32)],
        far=[columns, own, f1, b1, f2, b2, f3],
    )
    foreign = pair(foreign)
    share = [(share[i] + foreign[i].astype(F32)).astype(BF16) for i in range(4)]
    total = share[0].astype(F32)
    for step in (1, 3, 2):
        total += shift(share[step], "fsdp", 4, step).astype(F32)
    mine = total.astype(BF16)
    total = mine.astype(F32)
    for step in (1, 3, 2):
        total += shift(mine, "dp", 4, step).astype(F32)
    total = total.astype(BF16)
    p2, p6 = turn(total, 2), turn(total, -2)
    p1, p7 = turn(total, 1), turn(total, -1)
    p3, p4, p5 = turn(p2, 1), turn(p2, 2), turn(p6, -1)
    pieces = [total, p1, p2, p3, p4, p5, p6, p7]
    across = [pair(jnp.stack([pieces[i] for i in NEAR])), pair(jnp.stack([pieces[i] for i in FAR]))]
    shares = call(
        spread_kernel,
        ids,
        pieces + across,
        [((256, 512), F32)] * 4,
        [pltpu.VMEM((8, 128, 256), BF16)],
        shape=pltpu.HBM,
    )
    return (out[None], grad[None], *shares)


def solution(mesh):
    dp, seq, fsdp = mesh.devices.shape
    split = Mesh(mesh.devices.reshape(dp, seq // 2, 2, fsdp), ("dp", "z", "core", "fsdp"))
    frames = P(("dp", "fsdp"), ("z", "core"), None)
    rows = P("fsdp", None)

    return jax.shard_map(
        body,
        mesh=split,
        in_specs=(frames, rows, rows, rows, rows, frames),
        out_specs=(frames, frames, rows, rows, rows, rows),
        check_vma=False,
    )
```

```python
import jax
import jax.numpy as jnp
from jax import lax
from jax.experimental import pallas as pl
from jax.experimental.pallas import tpu as pltpu
from jax.sharding import Mesh
from jax.sharding import PartitionSpec as P


HSIZE = 64
LOG2E = 1.4426950408889634
F32 = jnp.float32
BF16 = jnp.bfloat16


def vmem(count):
    return [pl.BlockSpec(memory_space=pltpu.VMEM) for _ in range(count)]


def smem():
    return pl.BlockSpec(memory_space=pltpu.SMEM)


def call(kernel, ids, args, outs, scratch=(), limit=12, shape=(pltpu.VMEM,) * 4, far=()):
    spaces = [pltpu.VMEM] * len(args) + [pltpu.HBM] * len(far)
    args = [pltpu.with_memory_space_constraint(a, m) for a, m in zip([*args, *far], spaces)]
    return pl.pallas_call(
        kernel,
        in_specs=[smem()] + vmem(len(args)),
        out_specs=vmem(len(outs)),
        out_shape=[m(s, d) for m, (s, d) in zip(shape, outs)],
        scratch_shapes=list(scratch),
        compiler_params=pltpu.CompilerParams(vmem_limit_bytes=limit << 20),
    )(ids, *args)


def normalize(rows):
    wide = rows.astype(F32)
    centre = wide - jnp.mean(wide, axis=-1, keepdims=True)
    variance = jnp.mean(centre * centre, axis=-1, keepdims=True)
    inverse = lax.rsqrt(variance + 1e-05)
    return centre * inverse, inverse


def dot(a, b, dims):
    return lax.dot_general(a, b, (dims, ((), ())), preferred_element_type=F32)


def low_lanes(shape):
    return lax.broadcasted_iota(jnp.int32, shape, len(shape) - 1) < HSIZE


def shift(value, axis, size, by):
    return lax.ppermute(value, axis, [(i, (i + by) % size) for i in range(size)])


def pair(value):
    return shift(value, "core", 2, 1)


def block_of(ids, step):
    return pl.multiple_of(lax.rem(ids[1] + step, 4) * 256, 256)


def stack_kernel(ids, sig, up, both):
    both[0] = normalize(sig[...])[0].astype(BF16)
    both[1] = up[...]


def whole_weights(ids, pieces, whole):
    upper = pl.multiple_of(lax.rem(ids[3], 2) * 128, 128)
    lower = pl.multiple_of(128 - upper, 128)
    for step in range(4):
        whole[step, pl.ds(upper, 128), :] = pieces[2 * step][...]
        whole[step, pl.ds(lower, 128), :] = pieces[2 * step + 1][...]


def project_kernel(ids, own, oth, *refs):
    pieces, (heads, first, second, whole) = refs[:8], refs[8:]
    core = ids[0]
    whole_weights(ids, pieces, whole)
    for half, both in enumerate((own, oth)):
        at = core if half == 0 else 1 - core
        rows = pl.ds(pl.multiple_of(at * 128, 128), 128)
        first[rows, :] = both[0]
        second[rows, :] = jnp.where(core == 0, both[0], both[1])
    one = two = None
    for step in range(4):
        cols = pl.ds(block_of(ids, step), 256)
        a = dot(first[:, cols], whole[step, :, :512], ((1,), (0,)))
        b = dot(second[:, cols], whole[step, :, 512:], ((1,), (0,)))
        one = a if one is None else one + a
        two = b if two is None else two + b
    mask = low_lanes((256, 128))
    for pair in range(4):
        lanes = slice(128 * pair, 128 * pair + 128)
        t1, t2 = one[:, lanes], two[:, lanes]
        heads[2 * pair] = jnp.where(mask, t1, pltpu.roll(t2, 64, 1)).astype(BF16)
        heads[2 * pair + 1] = jnp.where(mask, pltpu.roll(t1, 64, 1), t2).astype(BF16)


def attend(kv, qg, turned_kv, acc, part, blocks):
    keys, block = kv.shape[0], 512
    low = low_lanes((keys, 128))
    zero = jnp.zeros((), BF16)
    pairs = kv[...]
    key_rows = jnp.where(low, pairs, zero)
    value_rows = jnp.where(low, zero, pairs)
    upper = lax.broadcasted_iota(jnp.int32, (128, keys), 0) < HSIZE
    columns = turned_kv[...]
    key_cols = jnp.where(upper, columns, zero)
    value_cols = jnp.where(upper, zero, columns)
    low_q = low_lanes((block, 128))
    scale = jnp.where(low_lanes((1, 128)), HSIZE**-0.5, 1.0).astype(F32)

    def step(i, carry):
        start = pl.multiple_of(i * block, block)
        qb = qg[pl.ds(start, block), :]
        s = dot(key_rows, qb, ((1,), (1,)))
        top = jnp.max(s, axis=0, keepdims=True)
        e = jnp.exp2((s - top) * (HSIZE**-0.5 * LOG2E))
        inv = 1.0 / jnp.sum(e, axis=0, keepdims=True)
        att = e * inv
        grad = dot(value_rows, qb, ((1,), (1,)))
        delta = jnp.sum(att * grad, axis=0, keepdims=True)
        weights = att.astype(BF16)
        gs = (att * (grad - delta)).astype(BF16)
        qk = jnp.where(low_q, qb, zero)
        qv = jnp.where(low_q, zero, qb)
        both, queries = jnp.concatenate([gs, weights], axis=1), jnp.concatenate([qk, qv], axis=0)
        acc[...] += dot(both, queries, ((1,), (0,)))
        turned = dot(key_cols, gs, ((1,), (0,))) + dot(value_cols, weights, ((1,), (0,)))
        part[pl.ds(start, block), :] = (turned.T * scale).astype(BF16)
        return carry

    lax.fori_loop(*blocks, step, 0)
    return scale


def attention_kernel(ids, own, other, send, keep, kv, qg, turned_kv, part):
    core, keys = ids[0], kv.shape[0]

    @pl.when(core == 0)
    def _():
        kv[...] = own[...]
        qg[...] = other[0:1024, :]

    @pl.when(core != 0)
    def _():
        kv[...] = other[...]
        qg[...] = own[1024:2048, :]

    turned_kv[...] = kv[...].astype(F32).T.astype(BF16)
    keep[...] = jnp.zeros_like(keep)
    scale = attend(kv, qg, turned_kv, keep, part, (0, 2))
    total = keep[...] * scale
    keep[...] = total
    send[0:keys, :] = total.astype(BF16)
    send[keys:, :] = part[...]


def merge_kernel(ids, keep, send, recv, moved, columns):
    core = ids[0]
    keys = keep.shape[0]
    half = keys // 2
    kv = (keep[...] + recv[0:keys, :].astype(F32)).astype(BF16)
    own, oth = send[keys:, :], recv[keys:, :]
    low = jnp.where(core == 0, own, oth)
    high = jnp.where(core == 0, oth, own)
    columns[:, 0:128] = kv
    columns[0:half, 128:256] = low
    columns[half:keys, 128:256] = high
    moved[0:half, :] = jnp.where(core == 0, kv[0:half], low)
    moved[half:keys, :] = jnp.where(core == 0, kv[half:keys], high)


def unpack(heads):
    mask = low_lanes((256, 128))
    one, two = [], []
    for pair in range(4):
        a, b = heads[2 * pair].astype(F32), heads[2 * pair + 1].astype(F32)
        one.append(jnp.where(mask, a, pltpu.roll(b, 64, 1)).astype(BF16))
        two.append(jnp.where(mask, pltpu.roll(a, 64, 1), b).astype(BF16))
    return jnp.concatenate(one, axis=1), jnp.concatenate(two, axis=1)


def outer_kernel(ids, columns, b3, f4, x0, f1, b1, f2, b2, f3, keep, send, acc_n, acc_u):
    core, place = ids[0], ids[2]

    def chunk(step):
        block = lax.rem(place + jnp.where(core == 0, 8 - step, step), 8)
        start = block * 256 + core * 128
        return columns[pl.ds(pl.multiple_of(start, 128), 128), :]

    for index, (low, high, a, b) in enumerate(
        ((0, 4, x0, f4), (1, 7, f1, b1), (2, 6, f2, b2), (3, 5, f3, b3))
    ):
        rows = jnp.concatenate([chunk(low), chunk(high)], axis=0)
        normed = jnp.concatenate([a[0], b[0]], axis=0)
        frames = jnp.concatenate([a[1], b[1]], axis=0)
        n, u = dot(normed, rows, ((0,), (0,))), dot(frames, rows[:, 128:], ((0,), (0,)))
        acc_n[...] = n if index == 0 else acc_n[...] + n
        acc_u[...] = u if index == 0 else acc_u[...] + u
    mask = low_lanes((128, 128))
    for step in range(4):
        base = block_of(ids, step)
        for half in range(2):
            rows = pl.ds(pl.multiple_of(base + half * 128, 128), 128)
            upper = jnp.where(mask, acc_n[rows, 128:], acc_u[rows, :])
            value = jnp.concatenate([acc_n[rows, :128], upper], axis=1)

            @pl.when(core == half)
            def _():
                keep[step] = value

            @pl.when(core != half)
            def _():
                send[step] = value.astype(BF16)


def back_kernel(ids, heads, *refs):
    pieces, (keep, send, whole) = refs[:8], refs[8:]
    core = ids[0]
    one, two = unpack(heads)
    whole_weights(ids, pieces, whole)
    for step in range(4):
        cols = pl.ds(block_of(ids, step), 256)
        a = dot(one, whole[step, :, :512], ((1,), (1,)))
        b = dot(two, whole[step, :, 512:], ((1,), (1,)))
        total = jnp.where(core == 0, a + b, a)
        extra = jnp.where(core == 0, 0.0, b)
        keep[0, :, cols] = jnp.where(core == 0, total[:128], total[128:])
        keep[1, :, cols] = jnp.where(core == 0, extra[:128], extra[128:])
        send[0, :, cols] = jnp.where(core == 0, total[128:], total[:128])
        send[1, :, cols] = jnp.where(core == 0, extra[128:], extra[:128])


NEAR, FAR = (0, 1, 7, 2, 6), (3, 4, 5)


def spread_kernel(ids, *refs):
    own, (near, far), (gq, gk, gv, go, heads) = refs[:8], refs[8:10], refs[10:]
    oth = {step: near.at[i] for i, step in enumerate(NEAR)}
    oth.update({step: far.at[i] for i, step in enumerate(FAR)})
    core, place = ids[0], ids[2]
    mask = low_lanes((128, 128))
    scale = 32768**-0.5
    for half, pieces in enumerate((own, oth)):
        for step in range(8):
            back = core if half == 1 else 1 - core
            heads[lax.rem(place + jnp.where(back == 1, 8 - step, step), 8)] = pieces[step][...]
        start = jnp.where(core == half, 0, 128)
        rows = pl.ds(pl.multiple_of(start, 128), 128)
        for duo in range(4):
            a, b = (heads[h].astype(F32) * scale for h in (2 * duo, 2 * duo + 1))
            lanes = slice(128 * duo, 128 * duo + 128)
            for first, (low, high) in ((0, (gk, gv)), (128, (gq, go))):
                ta, tb = a[:, first : first + 128], b[:, first : first + 128]
                low[rows, lanes] = jnp.where(mask, ta, pltpu.roll(tb, 64, 1))
                high[rows, lanes] = jnp.where(mask, pltpu.roll(ta, 64, 1), tb)


def finish_kernel(ids, sig, up, keep, recv, out, grad):
    normed_f, inverse = normalize(sig[...])
    out[...] = (sig[...].astype(F32) + keep[1] + recv[1]).astype(BF16)
    gn = keep[0] + recv[0]
    mean = jnp.mean(gn, axis=-1, keepdims=True)
    along = jnp.mean(gn * normed_f, axis=-1, keepdims=True)
    grad[...] = (up[...].astype(F32) + inverse * (gn - mean - normed_f * along)).astype(BF16)


def turn(value, by):
    perm = [(2 * i, 2 * ((i + by) % 8)) for i in range(8)]
    perm += [(2 * i + 1, 2 * ((i - by) % 8) + 1) for i in range(8)]
    return lax.ppermute(value, ("z", "core"), perm)


def exchange(value, axis):
    return lax.all_to_all(value, axis, split_axis=0, concat_axis=0, tiled=True)


def body(signal, w_query, w_key, w_value, w_output, upstream):
    core, place = lax.axis_index("core"), lax.axis_index("fsdp")
    ids = jnp.stack([core, place, lax.axis_index("z"), lax.axis_index("dp")]).astype(jnp.int32)
    sig, up = signal[0], upstream[0]
    w0 = jnp.concatenate(
        [jnp.where(core == 0, w_key, w_query), jnp.where(core == 0, w_value, w_output)], axis=1
    )
    even = lax.rem(lax.axis_index("dp"), 2) == 0
    w0a = jnp.where(even, w0[:128], w0[128:])
    w0b = jnp.where(even, w0[128:], w0[:128])
    w1a, w3b = shift(w0a, "fsdp", 4, -1), shift(w0b, "fsdp", 4, 1)
    (own,) = call(stack_kernel, ids, [sig, up], [((2, 128, 1024), BF16)])
    oth = pair(own)
    w2a, w1b = shift(w1a, "fsdp", 4, -1), shift(w1a, "dp", 4, -1)
    w2b, w3a = shift(w3b, "fsdp", 4, 1), shift(w3b, "dp", 4, 1)
    weights = [w0a, w0b, w1a, w1b, w2a, w2b, w3a, w3b]
    f1, b1 = turn(own, 1), turn(own, -1)
    f2, b2 = turn(f1, 1), turn(b1, -1)
    f3, b3 = turn(f2, 1), turn(b2, -1)
    f4 = turn(f3, 1)
    heads, _, _ = call(
        project_kernel,
        ids,
        [own, oth] + weights,
        [((8, 256, 128), BF16), ((256, 1024), BF16), ((256, 1024), BF16)],
        [pltpu.VMEM((4, 256, 1024), BF16)],
    )
    mine = exchange(heads, "z").reshape(2048, 128)
    other = pair(mine)
    send, keep = call(
        attention_kernel,
        ids,
        [mine, other],
        [((3072, 128), BF16), ((2048, 128), F32)],
        [
            pltpu.VMEM((2048, 128), BF16),
            pltpu.VMEM((1024, 128), BF16),
            pltpu.VMEM((128, 2048), BF16),
            pltpu.VMEM((1024, 128), BF16),
        ],
        30,
    )
    recv = pair(send)
    moved, columns = call(
        merge_kernel,
        ids,
        [keep, send, recv],
        [((2048, 128), BF16), ((2048, 256), BF16)],
        shape=(pltpu.HBM, pltpu.VMEM),
    )
    grads = exchange(moved.reshape(8, 256, 128), "z")
    kept, sent = call(
        back_kernel,
        ids,
        [grads],
        [((2, 128, 1024), F32), ((2, 128, 1024), F32)],
        [pltpu.VMEM((4, 256, 1024), BF16)],
        far=weights,
    )
    got = pair(sent)
    out, grad = call(
        finish_kernel,
        ids,
        [sig, up, kept, got],
        [((128, 1024), BF16), ((128, 1024), BF16)],
        shape=(pltpu.HBM,) * 4,
    )
    share, foreign = call(
        outer_kernel,
        ids,
        [columns, b3, f4],
        [((4, 128, 256), F32), ((4, 128, 256), BF16)],
        [pltpu.VMEM((1024, 256), F32), pltpu.VMEM((1024, 128), F32)],
        far=[own, f1, b1, f2, b2, f3],
    )
    foreign = pair(foreign)
    share = [(share[i] + foreign[i].astype(F32)).astype(BF16) for i in range(4)]
    total = share[0].astype(F32)
    for step in (1, 3, 2):
        total += shift(share[step], "fsdp", 4, step).astype(F32)
    mine = total.astype(BF16)
    total = mine.astype(F32)
    for step in (1, 3, 2):
        total += shift(mine, "dp", 4, step).astype(F32)
    total = total.astype(BF16)
    p2, p6 = turn(total, 2), turn(total, -2)
    p1, p7 = turn(total, 1), turn(total, -1)
    p3, p4, p5 = turn(p2, 1), turn(p2, 2), turn(p6, -1)
    pieces = [total, p1, p2, p3, p4, p5, p6, p7]
    across = [pair(jnp.stack([pieces[i] for i in NEAR])), pair(jnp.stack([pieces[i] for i in FAR]))]
    shares = call(
        spread_kernel,
        ids,
        pieces + across,
        [((256, 512), F32)] * 4,
        [pltpu.VMEM((8, 128, 256), BF16)],
        shape=(pltpu.HBM,) * 4,
    )
    return (out[None], grad[None], *shares)


def solution(mesh):
    dp, seq, fsdp = mesh.devices.shape
    split = Mesh(mesh.devices.reshape(dp, seq // 2, 2, fsdp), ("dp", "z", "core", "fsdp"))
    frames = P(("dp", "fsdp"), ("z", "core"), None)
    rows = P("fsdp", None)

    return jax.shard_map(
        body,
        mesh=split,
        in_specs=(frames, rows, rows, rows, rows, frames),
        out_specs=(frames, frames, rows, rows, rows, rows),
        check_vma=False,
    )
```
